256 devices in a mesh: enc: 4 (over z_lo), lab: 64 (over z_hi, y, x, core).
Axes of the slice: x: 4, y: 4, z: 8 (z_hi: 2, z_lo: 4; z = z_hi * 4 + z_lo), core: 2. Of those that a mesh axis runs over, the one named last changes fastest.
Arguments:
- embeddings: bfloat16 [131072, 768], P(('enc', 'lab')), may hold values from -6 to 6
- classifier: float32 [4096, 768], P('lab'), may hold values from -0.21875 to 0.21875
- label_valid: int32 [4096], P('lab'), may hold values 0 or 1
- shortlist: int32 [131072, 4], P(('enc', 'lab')), may hold values from 0 to 63, all different within a row; in each aligned block of 512 rows (0 to 511, 512 to 1023, ...) at most 48 rows name the same one
- slot_live: int32 [131072, 4], P(('enc', 'lab')), may hold values 0 or 1
- positive: int32 [131072, 4], P(('enc', 'lab')), may hold values from 0 to 63
- negative: int32 [131072, 4, 8], P(('enc', 'lab')), may hold values from 0 to 63
Outputs:
- w_grad: float32 [4096, 768], P('lab')
- emb_grad: float32 [131072, 768], P(('enc', 'lab'))
The draws below stay inside these ranges and needn't reach their ends.
Inputs may be any that keep to these rules, and one draw needn't show every extreme that they name: `shortlist`: each document names 4 different clusters; among the 512 documents of one device no cluster is named by more than 48 documents.
All inputs are finite; a program needn't handle non-finite values. No bound on the sum of `label_valid` or of `slot_live` on one device may be relied on, other than what follows from the above.
Results may differ from the reference program's by a relative error of at most 0.0041.
Values may be sent and summed in bfloat16 or wider, within the bound.
A program may use at most 128 MiB of HBM per device.

```python
import math
import jax
import jax.numpy as jnp
import numpy as np
from jax import lax

D = 768
PANEL = 64
S = 4
NNEG = 8
DOC_DEV = 512
CLUSTERS = 64
LABELS = 4096
DOCS = 131072
CAP = 48
ROUTED = 8192


def set_ends(entries, stream_key, least, largest):
    longest = entries.shape.index(max(entries.shape))
    spots = []
    for shift in (0, 1):
        where = [jax.random.randint(jax.random.fold_in(stream_key, axis), (), 0, length) for axis, length in enumerate(entries.shape)]
        where[longest] = (where[longest] + shift) % entries.shape[longest]
        spots.append(tuple(where))
    return entries.at[spots[0]].set(least).at[spots[1]].set(largest)


def level_of(rng, dims, shards, low, top_value):
    factor_of = 1.0
    for dim, blocks in shards:
        heights = jax.random.uniform(jax.random.fold_in(jax.random.fold_in(rng, 6), dim), (blocks,), jnp.float32, low / len(shards), top_value / len(shards))
        factor_of = factor_of * jnp.repeat(jnp.exp(heights), dims[dim] // blocks).reshape((-1,) + (1,) * (len(dims) - 1 - dim))
    return factor_of


def deal_out(own_key, own, number, rows, amount, top, reach, slope):
    order = jax.random.permutation(own_key, amount)
    crowded, usual = load_shares(amount, rows * top, reach, slope, True), load_shares(amount, rows * top, reach, slope, False)
    places = jnp.arange(amount)

    def named(sizes, offset_by):
        used = int((sizes > 0).sum())
        fixed = max(1, used // 4)
        moved = fixed + (places - fixed + offset_by * (used - fixed)) % max(1, amount - fixed)
        return jnp.zeros((amount,), jnp.int32).at[order[jnp.where(places < fixed, places, moved)]].set(jnp.asarray(sizes, jnp.int32))

    sizes = jnp.where(number % 4 == 0, named(crowded, number // 4), named(usual, number - number // 4 - 1))
    mixed = jax.random.permutation(jax.random.fold_in(own, 3), amount)
    source_of, receiver = mixed[0:amount // 2 * 2:2], mixed[1:amount // 2 * 2:2]
    room = jnp.minimum(sizes[source_of] - 1, reach - sizes[receiver]) // 2
    room = jnp.where((source_of == order[0]) | (receiver == order[0]) | (sizes[receiver] == 0), 0, jnp.maximum(room, 0))
    moved = jax.random.randint(jax.random.fold_in(own, 4), (amount // 2,), 0, 1 << 20) % (room + 1)
    sizes = sizes.at[source_of].add(-moved).at[receiver].add(moved)
    members = jnp.searchsorted(jnp.cumsum(sizes), jnp.arange(rows * top), side="right").astype(jnp.int32)
    table = members.reshape(top, rows).T
    table = table[jax.random.permutation(jax.random.fold_in(own, 1), rows)]
    offset_by = jax.random.randint(jax.random.fold_in(own, 2), (rows, 1), 0, top)
    return jnp.take_along_axis(table, (jnp.arange(top)[None, :] + offset_by) % top, axis=1)


def load_shares(number_of, total, reach, skew, full):
    weights = [(1 << 20) // math.isqrt(rank ** skew) + 1 for rank in range(1, number_of + 1)]
    largest = reach if full else min(reach, max(-(-total // number_of), total * weights[0] // sum(weights)))
    least = 1 if total - largest >= number_of - 1 else 0
    holding, rest = [largest] + [least] * (number_of - 1), total - largest - least * (number_of - 1)
    while rest > 0:
        movable = [i for i in range(1, number_of) if holding[i] < largest] or [i for i in range(1, number_of) if holding[i] < reach]
        mass, remaining = sum([weights[i] for i in movable]), rest
        for i in movable:
            addition = min(reach - holding[i], max(1, remaining * weights[i] // mass), rest)
            holding[i] = holding[i] + addition
            rest = rest - addition
    return np.array(holding)


def scatter_about(rng, extent, width, reach, cuts=(), kind=jnp.bfloat16):
    result = width * jax.random.normal(rng, extent, jnp.float32)
    if cuts:
        result = result * level_of(rng, extent, cuts, -0.22, 0.18)
    return jnp.clip(result, -reach, reach).astype(kind)


def setup_inputs(seed: int = 0) -> dict:
    splits = jax.random.split(jax.random.key(seed), 8)
    embeddings = scatter_about(splits[0], (DOCS, D), 1.0, 6.0, ((0, 256),))
    classifier = scatter_about(splits[1], (LABELS, D), D ** -0.5, 0.21875, ((0, 64),), jnp.float32)
    label_valid = set_ends((jax.random.randint(splits[2], (LABELS,), 0, 16) < 15).astype(jnp.int32), jax.random.fold_in(splits[2], 1), 0, 1)
    shortlist_keys = jax.random.split(jax.random.fold_in(splits[3], 1), DOCS // DOC_DEV)
    shortlist_turns = jax.random.permutation(jax.random.fold_in(splits[3], 3), DOCS // DOC_DEV)
    shortlist = jax.vmap(lambda own, number: deal_out(jax.random.fold_in(splits[3], 2), own, number, DOC_DEV, CLUSTERS, S, CAP, 2))(shortlist_keys, shortlist_turns).reshape((DOCS, S))
    slot_live = set_ends((jax.random.randint(splits[4], (DOCS, S), 0, 8) < 7).astype(jnp.int32), jax.random.fold_in(splits[4], 1), 0, 1)
    positive = set_ends(jax.random.randint(splits[5], (DOCS, S), 0, PANEL), jax.random.fold_in(splits[5], 1), 0, PANEL - 1).astype(jnp.int32)
    negative = set_ends(jax.random.randint(splits[6], (DOCS, S, NNEG), 0, PANEL), jax.random.fold_in(splits[6], 1), 0, PANEL - 1).astype(jnp.int32)
    return {"embeddings": embeddings, "classifier": classifier, "label_valid": label_valid, "shortlist": shortlist, "slot_live": slot_live, "positive": positive, "negative": negative}


def dense_targets(shortlist, slot_live, positive, negative):
    labels = jnp.arange(PANEL, dtype=jnp.int32)
    pos_hot = (positive[..., None] == labels).astype(jnp.float32)
    neg_count = lax.optimization_barrier(jnp.sum((negative[..., None] == labels).astype(jnp.float32), axis=2))
    live = slot_live.astype(jnp.float32)[..., None]
    slot_weight = live * (pos_hot + neg_count)
    cluster_hot = (shortlist[..., None] == jnp.arange(CLUSTERS, dtype=jnp.int32)).astype(jnp.float32)
    count = shortlist.shape[0]
    weight = jnp.einsum('nsc,nsj->ncj', cluster_hot, slot_weight).reshape(count, LABELS)
    target = jnp.einsum('nsc,nsj->ncj', cluster_hot, pos_hot).reshape(count, LABELS)
    return (weight, target)

def reference(embeddings, classifier, label_valid, shortlist, slot_live, positive, negative):
    classifier_b = classifier.astype(jnp.bfloat16)
    valid = label_valid.astype(jnp.float32)
    blocks = DOCS // DOC_DEV
    emb_blocks = embeddings.reshape(blocks, DOC_DEV, D)
    short_blocks = shortlist.reshape(blocks, DOC_DEV, S)
    live_blocks = slot_live.reshape(blocks, DOC_DEV, S)
    pos_blocks = positive.reshape(blocks, DOC_DEV, S)
    neg_blocks = negative.reshape(blocks, DOC_DEV, S, NNEG)

    def one_block(total, inputs):
        emb_b, short_b, live_b, pos_b, neg_b = inputs
        weight, target = dense_targets(short_b, live_b, pos_b, neg_b)
        weight = weight * valid[None, :]
        logits = lax.dot_general(emb_b, classifier_b, (((1,), (1,)), ((), ())), preferred_element_type=jnp.float32)
        dlogits = (weight * (jax.nn.sigmoid(logits) - target)).astype(jnp.bfloat16)
        emb_grad = jnp.dot(dlogits, classifier_b, preferred_element_type=jnp.float32)
        total = total + lax.dot_general(dlogits, emb_b, (((0,), (0,)), ((), ())), preferred_element_type=jnp.float32)
        return (total, emb_grad)
    start = jnp.zeros((LABELS, D), jnp.float32)
    total, emb_grads = lax.scan(one_block, start, (emb_blocks, short_blocks, live_blocks, pos_blocks, neg_blocks))
    w_grad = total * (1.0 / math.sqrt(ROUTED))
    return (w_grad, emb_grads.reshape(DOCS, D))
```

```python
import functools
import math

import jax
import jax.numpy as jnp
from jax import lax
from jax.experimental import pallas as pl
from jax.experimental.pallas import tpu as pltpu
from jax.sharding import PartitionSpec as P

MESH = pl.DeviceIdType.MESH
NT = (((1,), (1,)), ((), ()))
TN = (((0,), (0,)), ((), ()))


def rem4(v):
    return lax.rem(v + 8, 4)


class Place:
    def __init__(self):
        self.e = lax.axis_index("enc")
        lab = lax.axis_index("lab")
        self.c = lax.rem(lab, 2)
        self.x = lax.rem(lax.div(lab, 2), 4)
        self.y = lax.rem(lax.div(lab, 8), 4)
        self.h = lax.div(lab, 32)
        self.z = self.h * 4 + self.e

    def lab_of(self, h, y, x, c):
        return ((h * 4 + y) * 4 + x) * 2 + c

    def along_x(self, k):
        return (self.e, self.lab_of(self.h, self.y, rem4(self.x + k), self.c))

    def along_y(self, k):
        return (self.e, self.lab_of(self.h, rem4(self.y + k), self.x, self.c))

    def sibling(self):
        return (self.e, self.lab_of(self.h, self.y, self.x, 1 - self.c))

    def mirror(self):
        return (3 - self.e, self.lab_of(1 - self.h, self.y, self.x, self.c))

    def z_of(self, k):
        return lax.rem(self.z + k, 8)

    def along_z(self, k):
        z = self.z_of(k)
        return (lax.rem(z, 4), self.lab_of(lax.div(z, 4), self.y, self.x, self.c))

    def along_enc(self, k):
        return (rem4(self.e + k), self.lab_of(self.h, self.y, self.x, self.c))


class Mail:
    def __init__(self, send, recv):
        self.send, self.recv, self.used, self.sent = send, recv, 0, []

    def post(self, src, dst, device):
        n = self.used
        self.used += 1
        copy = pltpu.make_async_remote_copy(
            src_ref=src,
            dst_ref=dst,
            send_sem=self.send.at[n],
            recv_sem=self.recv.at[n],
            device_id=device,
            device_id_type=MESH,
        )
        copy.start()
        self.sent.append(copy)
        return copy

    def finish(self):
        for copy in self.sent:
            copy.wait_send()


def gather_half(mail, at, own, rh):
    block = lambda ry, rx: own.at[rh, ry, rx]
    right, left, up, down = at.along_x(1), at.along_x(-1), at.along_y(1), at.along_y(-1)
    post = mail.post
    xr = post(block(0, 0), block(0, 3), right)
    yu = post(block(0, 0), block(3, 0), up)
    xl = post(block(0, 0), block(0, 1), left)
    yd = post(block(0, 0), block(1, 0), down)
    yield
    half = lambda ry, rx, k: own.at[rh, ry, rx, k]
    sub = lambda ry, rx, k: own.at[rh, ry, rx, :, k]
    quarter = lambda ry, rx, k, s: own.at[rh, ry, rx, k, s]
    xr.wait_recv()
    x2a = post(sub(0, 3, 0), sub(0, 2, 0), right)
    u3 = post(half(0, 3, 0), half(3, 3, 0), up)
    d3 = post(half(0, 3, 0), half(1, 3, 0), down)
    yield
    yu.wait_recv()
    y2a = post(sub(3, 0, 0), sub(2, 0, 0), up)
    r3 = post(half(3, 0, 1), half(3, 3, 1), right)
    l3 = post(half(3, 0, 1), half(3, 1, 1), left)
    yield
    xl.wait_recv()
    x2b = post(sub(0, 1, 1), sub(0, 2, 1), left)
    u1 = post(half(0, 1, 0), half(3, 1, 0), up)
    d1 = post(half(0, 1, 0), half(1, 1, 0), down)
    yield
    yd.wait_recv()
    y2b = post(sub(1, 0, 1), sub(2, 0, 1), down)
    r1 = post(half(1, 0, 1), half(1, 3, 1), right)
    l1 = post(half(1, 0, 1), half(1, 1, 1), left)
    yield
    x2a.wait_recv()
    x2b.wait_recv()
    u2 = post(half(0, 2, 0), half(3, 2, 0), up)
    d2 = post(half(0, 2, 0), half(1, 2, 0), down)
    y2a.wait_recv()
    y2b.wait_recv()
    r2 = post(half(2, 0, 1), half(2, 3, 1), right)
    l2 = post(half(2, 0, 1), half(2, 1, 1), left)
    yield
    last = []
    for rx, u in ((3, u3), (1, u1)):
        u.wait_recv()
        last.append(post(quarter(3, rx, 0, 0), quarter(2, rx, 0, 0), up))
    for ry, r in ((3, r3), (1, r1)):
        r.wait_recv()
        last.append(post(quarter(ry, 3, 1, 0), quarter(ry, 2, 1, 0), right))
    for rx, d in ((3, d3), (1, d1)):
        d.wait_recv()
        last.append(post(quarter(1, rx, 0, 1), quarter(2, rx, 0, 1), down))
    for ry, l in ((3, l3), (1, l1)):
        l.wait_recv()
        last.append(post(quarter(ry, 1, 1, 1), quarter(ry, 2, 1, 1), left))
    yield
    u2.wait_recv()
    last.append(post(quarter(3, 2, 0, 0), quarter(2, 2, 0, 0), up))
    r2.wait_recv()
    last.append(post(quarter(2, 3, 1, 0), quarter(2, 2, 1, 0), right))
    d2.wait_recv()
    last.append(post(quarter(1, 2, 0, 1), quarter(2, 2, 0, 1), down))
    l2.wait_recv()
    last.append(post(quarter(2, 1, 1, 1), quarter(2, 2, 1, 1), left))
    yield
    for copy in last:
        copy.wait_recv()


class RingSum:
    def __init__(self, mail, send, recv, groups, value, plus, minus):
        self.mail, self.out, self.into, self.groups, self.value = mail, send, recv, groups, value
        self.plus, self.minus = plus, minus
        self.copies = {}

    def fill(self, way, slot, make):
        def one(g, carry):
            self.out[way, slot, g] = make(g).astype(jnp.bfloat16)
            return carry

        lax.fori_loop(0, self.groups, one, 0)
        self.copies[way, slot] = self.mail.post(
            self.out.at[way, slot], self.into.at[way, slot], self.plus if way == 0 else self.minus
        )

    def far(self):
        self.fill(0, 0, lambda g: self.value(g, 2, 0))
        self.fill(1, 0, lambda g: self.value(g, 2, 1))

    def near(self):
        self.fill(0, 1, lambda g: self.value(g, 1, 1))
        self.fill(1, 1, lambda g: self.value(g, 3, 0))

    def got(self, way, slot, g):
        return self.into[way, slot, g].astype(jnp.float32)

    def relay(self):
        self.copies[0, 0].wait_recv()
        self.fill(0, 2, lambda g: self.value(g, 1, 0) + self.got(0, 0, g))
        self.copies[1, 0].wait_recv()
        self.fill(1, 2, lambda g: self.value(g, 3, 1) + self.got(1, 0, g))

    def collect(self, store):
        for way in (0, 1):
            for slot in (1, 2):
                self.copies[way, slot].wait_recv()

        def one(g, carry):
            store(g, 0, self.value(g, 0, 0) + self.got(0, 2, g) + self.got(1, 1, g))
            store(g, 1, self.value(g, 0, 1) + self.got(0, 1, g) + self.got(1, 2, g))
            return carry

        lax.fori_loop(0, self.groups, one, 0)


def slot_weights(short_ref, live_ref, pos_ref, neg_ref, sw, panel, slots, nneg):
    docs = pos_ref.shape[1]
    label = lax.broadcasted_iota(jnp.int32, (panel, docs), 0)
    for s in range(slots):
        hot = jnp.where(pos_ref[pl.ds(s, 1), :] == label, 1.0, 0.0)
        count = hot
        for k in range(nneg):
            count += jnp.where(neg_ref[pl.ds(s * nneg + k, 1), :] == label, 1.0, 0.0)
        half = 0.5 * live_ref[pl.ds(s, 1), :].astype(jnp.float32)
        sw[s] = half * count * (1.0 - 2.0 * hot)


def kernel(
    scale, panel, slots, nneg,
    emb_ref, cls_ref, valid_ref, short_ref, live_ref, pos_ref, neg_ref,
    wg_ref, eg_ref,
    G, embh, sw, K, sib_out, sib_in,
    a1_out, a1_in, b1_out, b1_in, sum_a, sum_b, a2_out, a2_in, b2_out, b2_in,
    V, z_out, z_in, part,
    send, recv, sib_send, sib_recv,
):
    at = Place()
    width = emb_ref.shape[1]
    barrier = pltpu.get_barrier_semaphore()
    partners = [at.along_x(1), at.along_x(-1), at.along_y(1), at.along_y(-1), at.sibling()]
    partners += [at.along_z(k) for k in range(1, 8)]
    for device in partners:
        pl.semaphore_signal(barrier, inc=1, device_id=device, device_id_type=MESH)

    rows = lax.broadcasted_iota(jnp.int32, (panel, panel), 0)
    cols = lax.broadcasted_iota(jnp.int32, (panel, panel), 1)
    flags = jnp.where(rows == cols, valid_ref[...].astype(jnp.float32), 0.0)
    valid = jnp.sum(flags, axis=1, keepdims=True)
    mine = (cls_ref[...] * valid).astype(jnp.bfloat16)
    G[0, 0, 0, 0] = mine.reshape(2, 2, 16, width)
    pl.semaphore_wait(barrier, len(partners))

    mail = Mail(send, recv)
    own = G.at[0]
    mirrored = mail.post(own.at[0, 0, 0], own.at[1, 0, 0], at.mirror())
    near = gather_half(mail, at, own, 0)
    next(near)
    embh[...] = emb_ref[...] * jnp.bfloat16(0.5)
    slot_weights(short_ref, live_ref, pos_ref, neg_ref, sw, panel, slots, nneg)
    for _ in range(4):
        next(near)
    mirrored.wait_recv()
    other = gather_half(mail, at, own, 1)
    next(other)
    to_sibling = []

    def hand_over(rh, first, last):
        to_sibling.append(
            mail.post(G.at[0, rh, pl.ds(first, last - first)], G.at[1, rh, pl.ds(first, last - first)], at.sibling())
        )

    for _ in near:
        next(other, None)
    hand_over(0, 0, 4)
    for _ in other:
        pass
    hand_over(1, 0, 4)
    for copy in to_sibling:
        copy.wait_recv()

    eg_ref[...] = jnp.zeros_like(eg_ref)

    def score(rc, g):
        rh, ry = lax.div(g, 4), lax.rem(g, 4)
        w = G[rc, rh, ry].reshape(4 * panel, width)
        half_logits = lax.dot_general(w, embh[...], NT, preferred_element_type=jnp.float32)
        c = at.c if rc == 0 else 1 - at.c
        h = lax.rem(at.h + rh, 2)
        y = lax.rem(at.y + ry, 4)
        pieces = []
        for rx in range(4):
            cluster = at.lab_of(h, y, rem4(at.x + rx), c)
            hw = None
            for s in range(slots):
                term = sw[s] * jnp.where(short_ref[pl.ds(s, 1), :] == cluster, 1.0, 0.0)
                hw = term if hw is None else hw + term
            t = jnp.tanh(half_logits[rx * panel : (rx + 1) * panel])
            pieces.append((jnp.abs(hw) * t + hw).astype(jnp.bfloat16))
        dl = jnp.concatenate(pieces, axis=0)
        eg_ref[...] += lax.dot_general(dl, w, TN, preferred_element_type=jnp.float32)
        grad = jnp.dot(dl, emb_ref[...], preferred_element_type=jnp.float32)
        return rh, ry, grad.reshape(4, 2, 2, 16, width)

    def sibling_copy(g):
        rh, ry = lax.div(g, 4), lax.rem(g, 4)
        return pltpu.make_async_remote_copy(
            src_ref=sib_out.at[rh, ry],
            dst_ref=sib_in.at[rh, ry],
            send_sem=sib_send.at[g],
            recv_sem=sib_recv.at[g],
            device_id=at.sibling(),
            device_id_type=MESH,
        )

    def for_sibling(g, carry):
        rh, ry, grad = score(1, g)
        sib_out[rh, ry] = grad.astype(jnp.bfloat16)
        sibling_copy(g).start()
        return carry

    lax.fori_loop(0, 8, for_sibling, 0)

    def for_own(g, carry):
        rh, ry, grad = score(0, g)
        sibling_copy(g).wait_recv()
        K[rh, ry] = grad + sib_in[rh, ry].astype(jnp.float32)
        return carry

    lax.fori_loop(0, 8, for_own, 0)

    right, left, up, down = at.along_x(1), at.along_x(-1), at.along_y(1), at.along_y(-1)
    a1 = RingSum(
        mail, a1_out, a1_in, 8, lambda g, rel, s: K[lax.div(g, 4), lax.rem(g, 4), rel, 0, s], right, left
    )
    b1 = RingSum(
        mail, b1_out, b1_in, 8, lambda g, rel, s: K[lax.div(g, 4), rel, lax.rem(g, 4), 1, s], up, down
    )
    a1.far()
    b1.far()
    a1.near()
    b1.near()
    a1.relay()
    b1.relay()

    def store_a(g, s, v):
        sum_a[lax.div(g, 4), lax.rem(g, 4), s] = v

    def store_b(g, s, v):
        sum_b[lax.div(g, 4), lax.rem(g, 4), s] = v

    a1.collect(store_a)
    a2 = RingSum(mail, a2_out, a2_in, 2, lambda g, rel, s: sum_a[g, rel, s], up, down)
    a2.far()
    b1.collect(store_b)
    b2 = RingSum(mail, b2_out, b2_in, 2, lambda g, rel, s: sum_b[g, rel, s], right, left)
    b2.far()
    a2.near()
    b2.near()
    a2.relay()
    b2.relay()

    def store_va(g, s, v):
        V[g, s] = v
        z_out[g, s] = v.astype(jnp.bfloat16)

    def store_vb(g, s, v):
        V[g, 2 + s] = v
        z_out[g, 2 + s] = v.astype(jnp.bfloat16)

    a2.collect(store_va)
    b2.collect(store_vb)

    slices = []
    for k in range(1, 8):
        z = at.z_of(k)
        side = lax.rem(lax.div(z, 4) + at.h, 2)
        slices.append(mail.post(z_out.at[side, lax.rem(z, 4)], z_in.at[k - 1], at.along_z(k)))
    total = V[0, at.e]
    for k in range(1, 8):
        slices[k - 1].wait_recv()
        total += z_in[k - 1].astype(jnp.float32)
    part[at.e] = total * scale
    shares = [mail.post(part.at[at.e], part.at[at.e], at.along_enc(k)) for k in range(1, 4)]
    for copy in shares:
        copy.wait_recv()
    wg_ref[...] = part[...].reshape(panel, width) * valid

    mail.finish()

    def drain(g, carry):
        sibling_copy(g).wait_send()
        return carry

    lax.fori_loop(0, 8, drain, 0)


def shards(embeddings, classifier, label_valid, shortlist, slot_live, positive, negative):
    lab_count = lax.axis_size("lab")
    enc_count = lax.axis_size("enc")
    docs, width = embeddings.shape
    panel = classifier.shape[0]
    slots = shortlist.shape[1]
    nneg = negative.shape[2]
    scale = 1.0 / math.sqrt(docs * enc_count * slots)
    by_slot = lambda a: a.transpose(1, 0)
    vmem = pl.BlockSpec(memory_space=pltpu.VMEM)
    bf16, f32 = jnp.bfloat16, jnp.float32
    piece = (16, width)
    return pl.pallas_call(
        functools.partial(kernel, scale, panel, slots, nneg),
        out_shape=(
            jax.ShapeDtypeStruct((panel, width), f32),
            jax.ShapeDtypeStruct((docs, width), f32),
        ),
        in_specs=[vmem] * 7,
        out_specs=(vmem, vmem),
        scratch_shapes=[
            pltpu.VMEM((2, 2, 4, 4, 2, 2) + piece, bf16),
            pltpu.VMEM((docs, width), bf16),
            pltpu.VMEM((slots, panel, docs), f32),
            pltpu.VMEM((2, 4, 4, 2, 2) + piece, f32),
            pltpu.VMEM((2, 4, 4, 2, 2) + piece, bf16),
            pltpu.VMEM((2, 4, 4, 2, 2) + piece, bf16),
            pltpu.VMEM((2, 3, 8) + piece, bf16),
            pltpu.VMEM((2, 3, 8) + piece, bf16),
            pltpu.VMEM((2, 3, 8) + piece, bf16),
            pltpu.VMEM((2, 3, 8) + piece, bf16),
            pltpu.VMEM((2, 4, 2) + piece, f32),
            pltpu.VMEM((2, 4, 2) + piece, f32),
            pltpu.VMEM((2, 3, 2) + piece, bf16),
            pltpu.VMEM((2, 3, 2) + piece, bf16),
            pltpu.VMEM((2, 3, 2) + piece, bf16),
            pltpu.VMEM((2, 3, 2) + piece, bf16),
            pltpu.VMEM((2, 4) + piece, f32),
            pltpu.VMEM((2, 4) + piece, bf16),
            pltpu.VMEM((7,) + piece, bf16),
            pltpu.VMEM((4,) + piece, f32),
            pltpu.SemaphoreType.DMA((104,)),
            pltpu.SemaphoreType.DMA((104,)),
            pltpu.SemaphoreType.DMA((8,)),
            pltpu.SemaphoreType.DMA((8,)),
        ],
        compiler_params=pltpu.CompilerParams(
            collective_id=0, has_side_effects=True, vmem_limit_bytes=60 * 1024 * 1024
        ),
        name="step",
    )(
        embeddings,
        classifier,
        label_valid.reshape(1, panel),
        by_slot(shortlist),
        by_slot(slot_live),
        by_slot(positive),
        negative.transpose(1, 2, 0).reshape(slots * nneg, docs),
    )


def solution(mesh):
    in_specs = (
        P(("enc", "lab"), None),
        P("lab", None),
        P("lab"),
        P(("enc", "lab"), None),
        P(("enc", "lab"), None),
        P(("enc", "lab"), None),
        P(("enc", "lab"), None, None),
    )
    out_specs = (P("lab", None), P(("enc", "lab"), None))
    return jax.shard_map(shards, mesh=mesh, in_specs=in_specs, out_specs=out_specs, check_vma=False)
```

```python
import functools
import heapq
import math

import jax
import jax.numpy as jnp
from jax import lax
from jax.experimental import pallas as pl
from jax.experimental.pallas import tpu as pltpu
from jax.sharding import PartitionSpec as P

MESH = pl.DeviceIdType.MESH
NT = (((1,), (1,)), ((), ()))
TN = (((0,), (0,)), ((), ()))


def rem4(v):
    return lax.rem(v + 8, 4)


class Place:
    def __init__(self):
        self.e = lax.axis_index("enc")
        lab = lax.axis_index("lab")
        self.c = lax.rem(lab, 2)
        self.x = lax.rem(lax.div(lab, 2), 4)
        self.y = lax.rem(lax.div(lab, 8), 4)
        self.h = lax.div(lab, 32)

    def lab_of(self, h, y, x, c):
        return ((h * 4 + y) * 4 + x) * 2 + c

    def along_x(self, k):
        return (self.e, self.lab_of(self.h, self.y, rem4(self.x + k), self.c))

    def along_y(self, k):
        return (self.e, self.lab_of(self.h, rem4(self.y + k), self.x, self.c))

    def sibling(self):
        return (self.e, self.lab_of(self.h, self.y, self.x, 1 - self.c))

    def mirror(self):
        return (3 - self.e, self.lab_of(1 - self.h, self.y, self.x, self.c))

    def across(self, k):
        return (rem4(self.e + k), self.lab_of(1 - self.h, self.y, self.x, self.c))

    def along_enc(self, k):
        return (rem4(self.e + k), self.lab_of(self.h, self.y, self.x, self.c))


class Copy:
    def __init__(self, mail, n, src, dst, device):
        self.mail, self.n, self.src, self.dst, self.device = mail, n, src, dst, device

    def made(self):
        return pltpu.make_async_remote_copy(
            src_ref=self.src[0].at[self.src[1:]],
            dst_ref=self.dst[0].at[self.dst[1:]],
            send_sem=self.mail.send.at[self.n],
            recv_sem=self.mail.recv.at[self.n],
            device_id=self.device,
            device_id_type=MESH,
        )

    def wait_recv(self):
        self.made().wait_recv()


class Mail:
    def __init__(self, send, recv):
        self.send, self.recv, self.sent = send, recv, []

    def post(self, src, dst, device):
        copy = Copy(self, len(self.sent), src, dst, device)
        copy.made().start()
        self.sent.append(copy)
        return copy

    def finish(self):
        for copy in self.sent:
            copy.made().wait_send()


RIGHT, LEFT, UP, DOWN = range(4)


def onward(key):
    rh, k, s, ry, rx = key
    first, second = (rx, ry) if k == 0 else (ry, rx)
    ways = ((RIGHT, LEFT), (UP, DOWN)) if k == 0 else ((UP, DOWN), (RIGHT, LEFT))

    def there(f, t):
        return (rh, k, s, t, f) if k == 0 else (rh, k, s, f, t)

    out = []
    if second == 0:
        if first == 0:
            out += [(ways[0][0], there(3, 0)), (ways[0][1], there(1, 0))]
        if first == (1 if s else 3):
            out += [(ways[0][s], there(2, 0))]
        out += [(ways[1][0], there(first, 3)), (ways[1][1], there(first, 1))]
    if second == (1 if s else 3):
        out += [(ways[1][s], there(first, 2))]
    return out


def gather_plan(chunks, wire=0.55, hop=2.0, chunk_time=1.9):
    plan, events, free, now = [], [], [0.0] * 4, 0.0
    parts = [(k, s) for s in (0, 1) for k in (0, 1)]
    for n, (k, s) in enumerate(parts):
        heapq.heappush(events, (0.0, n, (0, k, s, 0, 0)))
        heapq.heappush(events, (4.0 + 1.05 * n, 4 + n, (1, k, s, 0, 0)))
    order, have = 8, set()
    todo = list(chunks)

    def runnable():
        for rh, k, pair in todo:
            firsts, seconds = (2 * pair, 2 * pair + 1), range(4)
            places = [(t, f) if k == 0 else (f, t) for f in firsts for t in seconds]
            if all((rh, k, s) + place in have for place in places for s in (0, 1)):
                return rh, k, pair
        return None

    while events or todo:
        chunk = runnable()
        quiet = not events or events[0][0] > now + 0.5 or min(free) > now + 1.5
        if chunk and quiet:
            todo.remove(chunk)
            plan.append(("chunk",) + chunk)
            now += chunk_time
            continue
        time, _, key = heapq.heappop(events)
        now = max(now, time) + 0.03
        plan.append(("wait", key))
        for way, then in onward(key):
            free[way] = max(now, free[way]) + wire
            heapq.heappush(events, (free[way] + hop, order, then))
            order += 1
            now += 0.03
            plan.append(("send", key, then, way))
        have.add(key)
    return plan


class RingSum:
    def __init__(self, mail, out, into, rh, groups, value, plus, minus):
        self.mail, self.out, self.into, self.rh, self.groups, self.value = mail, out, into, rh, groups, value
        self.plus, self.minus = plus, minus
        self.copies = {}

    def fill(self, way, slot, make):
        def one(g, carry):
            self.out[self.rh, way, slot, g] = make(g).astype(jnp.bfloat16)
            return carry

        lax.fori_loop(0, self.groups, one, 0, unroll=True)
        self.copies[way, slot] = self.mail.post(
            (self.out, self.rh, way, slot), (self.into, self.rh, way, slot), self.minus if way else self.plus
        )

    def far(self):
        self.fill(0, 0, lambda g: self.value(g, 2, 0))
        self.fill(1, 0, lambda g: self.value(g, 2, 1))

    def near(self, way):
        self.fill(way, 1, lambda g: self.value(g, 3 if way else 1, 0 if way else 1))

    def got(self, way, slot, g):
        return self.into[self.rh, way, slot, g].astype(jnp.float32)

    def relay(self, way):
        self.copies[way, 0].wait_recv()
        self.fill(way, 2, lambda g: self.value(g, 3 if way else 1, way) + self.got(way, 0, g))

    def collect(self, store):
        for way in (0, 1):
            for slot in (1, 2):
                self.copies[way, slot].wait_recv()

        def one(g, carry):
            store(g, 0, self.value(g, 0, 0) + self.got(0, 2, g) + self.got(1, 1, g))
            store(g, 1, self.value(g, 0, 1) + self.got(0, 1, g) + self.got(1, 2, g))
            return carry

        lax.fori_loop(0, self.groups, one, 0, unroll=True)


def slot_weights(live_ref, pos_ref, neg_ref, sw, side, panel, slots, nneg):
    docs = pos_ref.shape[1]
    label = lax.broadcasted_iota(jnp.int32, (panel, docs), 0)
    for s in range(slots):
        hot = jnp.where(pos_ref[pl.ds(s, 1), :] == label, 1.0, 0.0)
        count = hot
        for k in range(nneg):
            count += jnp.where(neg_ref[pl.ds(s * nneg + k, 1), :] == label, 1.0, 0.0)
        half = 0.5 * live_ref[pl.ds(s, 1), :].astype(jnp.float32)
        sw[side, s] = half * count * (1.0 - 2.0 * hot)


def kernel(
    scale, panel, slots, nneg,
    emb_ref, cls_ref, valid_ref, short_ref, live_ref, pos_ref, neg_ref,
    wg_ref, eg_ref,
    G, emb2, embh, sw, dl, K, eg, eg_in, short_in, live_in, pos_in, neg_in,
    a1_out, a1_in, b1_out, b1_in, sum_a, sum_b, a2_out, a2_in, b2_out, b2_in,
    V, z_out, z_in, part,
    send, recv,
):
    at = Place()
    docs, width = emb_ref.shape
    right, left, up, down = at.along_x(1), at.along_x(-1), at.along_y(1), at.along_y(-1)
    sibling = at.sibling()
    barrier = pltpu.get_barrier_semaphore()
    partners = [right, left, up, down, sibling]
    partners += [at.along_enc(k) for k in range(1, 4)] + [at.across(k) for k in range(4)]
    for device in partners:
        pl.semaphore_signal(barrier, inc=1, device_id=device, device_id_type=MESH)

    rows = lax.broadcasted_iota(jnp.int32, (panel, panel), 0)
    cols = lax.broadcasted_iota(jnp.int32, (panel, panel), 1)
    flags = jnp.where(rows == cols, valid_ref[...].astype(jnp.float32), 0.0)
    valid = jnp.sum(flags, axis=1, keepdims=True)
    mine = (cls_ref[...] * valid).astype(jnp.bfloat16)
    G[0, 0, 0] = mine.reshape(2, 2, 16, width)
    pl.semaphore_wait(barrier, len(partners))

    mail = Mail(send, recv)

    def score(rh, parts):
        blocks = []
        for k, pair in parts:
            rows = pl.ds(2 * pair, 2)
            block = G[rh, :, rows, 0] if k == 0 else G[rh, rows, :, 1]
            blocks.append(block.reshape(4 * panel, width))
        w = blocks[0] if len(blocks) == 1 else jnp.concatenate(blocks, axis=0)
        labels = w.shape[0]
        half_logits = lax.dot_general(w, embh[...], NT, preferred_element_type=jnp.float32)
        h = at.h if rh == 0 else 1 - at.h
        row = 0
        for k, pair in parts:
            for a in range(8):
                ry, rx = (a // 2, 2 * pair + a % 2) if k == 0 else (2 * pair + a // 4, a % 4)
                cluster = at.lab_of(h, rem4(at.y + ry), rem4(at.x + rx), at.c)
                for side, short in enumerate((short_ref, short_in)):
                    hw = None
                    for s in range(slots):
                        term = sw[side, s, pl.ds(k * panel // 2, panel // 2)] * jnp.where(
                            short[pl.ds(s, 1), :] == cluster, 1.0, 0.0
                        )
                        hw = term if hw is None else hw + term
                    t = jnp.tanh(half_logits[row : row + panel // 2, side * docs : (side + 1) * docs])
                    dl[pl.ds(row, panel // 2), pl.ds(side * docs, docs)] = (jnp.abs(hw) * t + hw).astype(jnp.bfloat16)
                row += panel // 2
        d = dl[pl.ds(0, labels), :]
        grad = jnp.dot(d, emb2[...], preferred_element_type=jnp.float32)
        for n, (k, pair) in enumerate(parts):
            rows = pl.ds(2 * pair, 2)
            part_grad = grad[n * 4 * panel : (n + 1) * 4 * panel]
            if k == 0:
                K[rh, :, rows, 0] = part_grad.reshape(4, 2, 2, 16, width)
            else:
                K[rh, rows, :, 1] = part_grad.reshape(2, 4, 2, 16, width)
        eg[...] += lax.dot_general(d, w, TN, preferred_element_type=jnp.float32)

    def term_a(rh):
        return lambda g, rel, s: K[rh, g, rel, 0, s]

    def term_b(rh):
        return lambda g, rel, s: K[rh, rel, g, 1, s]

    def ring(out, into, rh, groups, value, plus, minus):
        return RingSum(mail, out, into, rh, groups, value, plus, minus)

    a1 = [ring(a1_out, a1_in, rh, 4, term_a(rh), right, left) for rh in (0, 1)]
    b1 = [ring(b1_out, b1_in, rh, 4, term_b(rh), up, down) for rh in (0, 1)]
    a2 = [ring(a2_out, a2_in, rh, 1, lambda g, rel, s, rh=rh: sum_a[rh, rel, s], up, down) for rh in (0, 1)]
    b2 = [ring(b2_out, b2_in, rh, 1, lambda g, rel, s, rh=rh: sum_b[rh, rel, s], right, left) for rh in (0, 1)]

    def first_relays(rh, way):
        a1[rh].relay(way)
        b1[rh].relay(way)

    def first_far(rh):
        a1[rh].far()
        b1[rh].far()
        a1[rh].near(1)
        b1[rh].near(1)

    def first_near(rh):
        a1[rh].near(0)
        b1[rh].near(0)

    def second_sends(rh):
        def store_a(g, s, v):
            sum_a[rh, g, s] = v

        def store_b(g, s, v):
            sum_b[rh, g, s] = v

        a1[rh].collect(store_a)
        a2[rh].far()
        b1[rh].collect(store_b)
        b2[rh].far()
        for way in (0, 1):
            a2[rh].near(way)
            b2[rh].near(way)

    def second_relays(rh):
        for way in (0, 1):
            a2[rh].relay(way)
            b2[rh].relay(way)

    def plane_sum(rh):
        def store(half):
            def put(g, s, v):
                V[rh, 2 * half + s] = v
                z_out[rh, 2 * half + s] = v.astype(jnp.bfloat16)

            return put

        a2[rh].collect(store(0))
        b2[rh].collect(store(1))

    slices = []

    def z_sends(rh):
        for k in range(1 - rh, 4):
            device = at.across(k) if rh else at.along_enc(k)
            slices.append(mail.post((z_out, rh, rem4(at.e + k)), (z_in, len(slices)), device))

    posted = {}
    devices = (right, left, up, down)
    mirror = at.mirror()
    parts = [(k, s) for s in (0, 1) for k in (0, 1)]

    def piece(key):
        rh, k, s, ry, rx = key
        return (G, rh, ry, rx, k, s)

    def follow(plan):
        for what in plan:
            if what[0] == "chunk":
                score(what[1], [what[2:]])
            elif what[0] == "send":
                posted[what[2]] = mail.post(piece(what[1]), piece(what[2]), devices[what[3]])
            elif what[1] in posted:
                posted[what[1]].wait_recv()

    plan = gather_plan([(0, k, pair) for pair in (1, 0) for k in (0, 1)])
    opening = next(n for n, what in enumerate(plan) if what[0] == "wait" and (what[1][0] or what[1][3] or what[1][4]))
    follow(plan[:opening])
    for k, s in parts:
        posted[1, k, s, 0, 0] = mail.post((G, 0, 0, 0, k, s), (G, 1, 0, 0, k, s), mirror)
    whole = slice(None)
    shared = [
        mail.post((src, whole), (dst, whole), sibling)
        for src, dst in ((short_ref, short_in), (live_ref, live_in), (pos_ref, pos_in), (neg_ref, neg_in))
    ]
    shared.append(mail.post((emb_ref, whole), (emb2, pl.ds(docs, docs)), sibling))
    emb2[pl.ds(0, docs), :] = emb_ref[...]
    embh[pl.ds(0, docs), :] = emb_ref[...] * jnp.bfloat16(0.5)
    slot_weights(live_ref, pos_ref, neg_ref, sw, 0, panel, slots, nneg)
    eg[...] = jnp.zeros_like(eg)
    for copy in shared:
        copy.wait_recv()
    slot_weights(live_in, pos_in, neg_in, sw, 1, panel, slots, nneg)
    embh[pl.ds(docs, docs), :] = emb2[pl.ds(docs, docs), :] * jnp.bfloat16(0.5)
    follow(plan[opening:])
    first_far(0)
    first_near(0)
    score(1, [(0, 1), (1, 1)])
    first_relays(0, 0)
    first_relays(0, 1)
    first_far(1)
    score(1, [(0, 0), (1, 0)])
    returned = mail.post((eg, pl.ds(docs, docs)), (eg_in, whole), sibling)
    first_near(1)
    first_relays(1, 1)
    first_relays(1, 0)
    second_sends(0)
    second_relays(0)
    second_sends(1)
    plane_sum(0)
    z_sends(0)
    returned.wait_recv()
    eg_ref[...] = eg[pl.ds(0, docs), :] + eg_in[...]
    second_relays(1)
    plane_sum(1)
    z_sends(1)

    total = V[0, at.e]
    for k, copy in enumerate(slices):
        copy.wait_recv()
        total += z_in[k].astype(jnp.float32)
    part[at.e] = total * scale
    shares = [mail.post((part, at.e), (part, at.e), at.along_enc(k)) for k in range(1, 4)]
    for copy in shares:
        copy.wait_recv()
    wg_ref[...] = part[...].reshape(panel, width) * valid

    mail.finish()


def shards(embeddings, classifier, label_valid, shortlist, slot_live, positive, negative):
    lab_count = lax.axis_size("lab")
    enc_count = lax.axis_size("enc")
    docs, width = embeddings.shape
    panel = classifier.shape[0]
    slots = shortlist.shape[1]
    nneg = negative.shape[2]
    scale = 1.0 / math.sqrt(docs * enc_count * slots)
    by_slot = lambda a: a.transpose(1, 0)
    vmem = pl.BlockSpec(memory_space=pltpu.VMEM)
    bf16, f32 = jnp.bfloat16, jnp.float32
    piece = (16, width)
    return pl.pallas_call(
        functools.partial(kernel, scale, panel, slots, nneg),
        out_shape=(
            jax.ShapeDtypeStruct((panel, width), f32),
            jax.ShapeDtypeStruct((docs, width), f32),
        ),
        in_specs=[vmem] * 7,
        out_specs=(vmem, vmem),
        scratch_shapes=[
            pltpu.VMEM((2, 4, 4, 2, 2) + piece, bf16),
            pltpu.VMEM((2 * docs, width), bf16),
            pltpu.VMEM((2 * docs, width), bf16),
            pltpu.VMEM((2, slots, panel, docs), f32),
            pltpu.VMEM((8 * panel, 2 * docs), bf16),
            pltpu.VMEM((2, 4, 4, 2, 2) + piece, f32),
            pltpu.VMEM((2 * docs, width), f32),
            pltpu.VMEM((docs, width), f32),
            pltpu.VMEM((slots, docs), jnp.int32),
            pltpu.VMEM((slots, docs), jnp.int32),
            pltpu.VMEM((slots, docs), jnp.int32),
            pltpu.VMEM((slots * nneg, docs), jnp.int32),
            pltpu.VMEM((2, 2, 3, 4) + piece, bf16),
            pltpu.VMEM((2, 2, 3, 4) + piece, bf16),
            pltpu.VMEM((2, 2, 3, 4) + piece, bf16),
            pltpu.VMEM((2, 2, 3, 4) + piece, bf16),
            pltpu.VMEM((2, 4, 2) + piece, f32),
            pltpu.VMEM((2, 4, 2) + piece, f32),
            pltpu.VMEM((2, 2, 3, 1) + piece, bf16),
            pltpu.VMEM((2, 2, 3, 1) + piece, bf16),
            pltpu.VMEM((2, 2, 3, 1) + piece, bf16),
            pltpu.VMEM((2, 2, 3, 1) + piece, bf16),
            pltpu.VMEM((2, 4) + piece, f32),
            pltpu.VMEM((2, 4) + piece, bf16),
            pltpu.VMEM((7,) + piece, bf16),
            pltpu.VMEM((4,) + piece, f32),
            pltpu.SemaphoreType.DMA((192,)),
            pltpu.SemaphoreType.DMA((192,)),
        ],
        compiler_params=pltpu.CompilerParams(
            collective_id=0, has_side_effects=True, vmem_limit_bytes=60 * 1024 * 1024
        ),
        name="step",
    )(
        embeddings,
        classifier,
        label_valid.reshape(1, panel),
        by_slot(shortlist),
        by_slot(slot_live),
        by_slot(positive),
        negative.transpose(1, 2, 0).reshape(slots * nneg, docs),
    )


def solution(mesh):
    in_specs = (
        P(("enc", "lab"), None),
        P("lab", None),
        P("lab"),
        P(("enc", "lab"), None),
        P(("enc", "lab"), None),
        P(("enc", "lab"), None),
        P(("enc", "lab"), None, None),
    )
    out_specs = (P("lab", None), P(("enc", "lab"), None))
    return jax.shard_map(shards, mesh=mesh, in_specs=in_specs, out_specs=out_specs, check_vma=False)
```

```python
import functools
import heapq
import math

import jax
import jax.numpy as jnp
from jax import lax
from jax.experimental import pallas as pl
from jax.experimental.pallas import tpu as pltpu
from jax.sharding import PartitionSpec as P

MESH = pl.DeviceIdType.MESH
NT = (((1,), (1,)), ((), ()))
TN = (((0,), (0,)), ((), ()))


def rem4(v):
    return lax.rem(v + 8, 4)


class Place:
    def __init__(self):
        self.e = lax.axis_index("enc")
        lab = lax.axis_index("lab")
        self.c = lax.rem(lab, 2)
        self.x = lax.rem(lax.div(lab, 2), 4)
        self.y = lax.rem(lax.div(lab, 8), 4)
        self.h = lax.div(lab, 32)

    def lab_of(self, h, y, x, c):
        return ((h * 4 + y) * 4 + x) * 2 + c

    def along_x(self, k):
        return (self.e, self.lab_of(self.h, self.y, rem4(self.x + k), self.c))

    def along_y(self, k):
        return (self.e, self.lab_of(self.h, rem4(self.y + k), self.x, self.c))

    def sibling(self):
        return (self.e, self.lab_of(self.h, self.y, self.x, 1 - self.c))

    def mirror(self):
        return (3 - self.e, self.lab_of(1 - self.h, self.y, self.x, self.c))

    def across(self, k):
        return (rem4(self.e + k), self.lab_of(1 - self.h, self.y, self.x, self.c))

    def along_enc(self, k):
        return (rem4(self.e + k), self.lab_of(self.h, self.y, self.x, self.c))


class Copy:
    def __init__(self, mail, n, src, dst, device):
        self.mail, self.n, self.src, self.dst, self.device = mail, n, src, dst, device

    def made(self):
        return pltpu.make_async_remote_copy(
            src_ref=self.src[0].at[self.src[1:]],
            dst_ref=self.dst[0].at[self.dst[1:]],
            send_sem=self.mail.send.at[self.n],
            recv_sem=self.mail.recv.at[self.n],
            device_id=self.device,
            device_id_type=MESH,
        )

    def wait_recv(self):
        self.made().wait_recv()


class Mail:
    def __init__(self, send, recv):
        self.send, self.recv, self.sent = send, recv, []

    def post(self, src, dst, device):
        copy = Copy(self, len(self.sent), src, dst, device)
        copy.made().start()
        self.sent.append(copy)
        return copy

    def finish(self):
        for copy in self.sent:
            copy.made().wait_send()


RIGHT, LEFT, UP, DOWN = range(4)


def onward(key):
    rh, k, s, ry, rx = key
    first, second = (rx, ry) if k == 0 else (ry, rx)
    ways = ((RIGHT, LEFT), (UP, DOWN)) if k == 0 else ((UP, DOWN), (RIGHT, LEFT))

    def there(s, f, t):
        return (rh, k, s, t, f) if k == 0 else (rh, k, s, f, t)

    out = []
    if second == 0:
        if first == 0:
            out += [(ways[0][0], there(None, 3, 0), 4), (ways[0][1], there(None, 1, 0), 4)]
        elif first != 2:
            s = 0 if first == 3 else 1
            out += [(ways[0][s], there(s, 2, 0), 3)]
        out += [(ways[1][0], there(None, first, 3), 2), (ways[1][1], there(None, first, 1), 2)]
    elif second != 2:
        s = 0 if second == 3 else 1
        out += [(ways[1][s], there(s, first, 2), 1)]
    return out


def gather_plan(chunks, wire=0.6, hop=2.6, chunk_time=1.9):
    plan, free, now = [], [0.0] * 4, 0.0
    events = [(0.0, k, (0, k, None, 0, 0)) for k in (0, 1)] + [(5.0 + 2.0 * k, 2 + k, (1, k, None, 0, 0)) for k in (0, 1)]
    heapq.heapify(events)
    order, have, todo = 4, set(), list(chunks)

    def runnable():
        for rh, parts in todo:
            places = [(k, t, f) if k == 0 else (k, f, t) for k, f in parts for t in range(4)]
            if all((rh,) + place in have for place in places):
                return rh, parts
        return None

    while events or todo:
        chunk = runnable()
        quiet = not events or events[0][0] > now + 0.5 or min(free) > now + 1.5
        if chunk and quiet:
            todo.remove(chunk)
            plan.append(("chunk",) + chunk)
            now += chunk_time
            continue
        now = max(now, events[0][0])
        sends = []
        while events and events[0][0] <= now:
            key = heapq.heappop(events)[2]
            plan.append(("wait", key))
            now += 0.03
            rh, k, s, ry, rx = key
            if s is not None:
                if (rh, k, 1 - s, ry, rx) not in have:
                    have.add(key)
                    continue
                key = (rh, k, None, ry, rx)
            have.add((rh, k, ry, rx))
            sends += [(-left, rh, way, key, then) for way, then, left in onward(key)]
        for _, _, way, key, then in sorted(sends, key=lambda send: send[:3]):
            free[way] = max(now, free[way]) + (wire if then[2] is not None else 2 * wire)
            heapq.heappush(events, (free[way] + hop, order, then))
            order += 1
            now += 0.03
            plan.append(("send", key, then, way))
    return plan


class RingSum:
    def __init__(self, mail, out, into, rh, groups, value, plus, minus):
        self.mail, self.out, self.into, self.rh, self.groups, self.value = mail, out, into, rh, groups, value
        self.plus, self.minus = plus, minus
        self.copies = {}

    def fill(self, way, slot, make):
        def one(g, carry):
            self.out[self.rh, way, slot, g] = make(g).astype(jnp.bfloat16)
            return carry

        lax.fori_loop(0, self.groups, one, 0, unroll=True)
        self.copies[way, slot] = self.mail.post(
            (self.out, self.rh, way, slot), (self.into, self.rh, way, slot), self.minus if way else self.plus
        )

    def far(self):
        self.fill(0, 0, lambda g: self.value(g, 2, 0))
        self.fill(1, 0, lambda g: self.value(g, 2, 1))

    def near(self, way):
        self.fill(way, 1, lambda g: self.value(g, 3 if way else 1, 0 if way else 1))

    def got(self, way, slot, g):
        return self.into[self.rh, way, slot, g].astype(jnp.float32)

    def relay(self, way):
        self.copies[way, 0].wait_recv()
        self.fill(way, 2, lambda g: self.value(g, 3 if way else 1, way) + self.got(way, 0, g))

    def collect(self, store):
        for way in (0, 1):
            for slot in (1, 2):
                self.copies[way, slot].wait_recv()

        def one(g, carry):
            store(g, 0, self.value(g, 0, 0) + self.got(0, 2, g) + self.got(1, 1, g))
            store(g, 1, self.value(g, 0, 1) + self.got(0, 1, g) + self.got(1, 2, g))
            return carry

        lax.fori_loop(0, self.groups, one, 0, unroll=True)


def slot_weights(live_ref, pos_ref, neg_ref, sw, side, panel, slots, nneg):
    docs = pos_ref.shape[1]
    label = lax.broadcasted_iota(jnp.int32, (panel, docs), 0)
    for s in range(slots):
        hot = jnp.where(pos_ref[pl.ds(s, 1), :] == label, 1.0, 0.0)
        count = hot
        for k in range(nneg):
            count += jnp.where(neg_ref[pl.ds(s * nneg + k, 1), :] == label, 1.0, 0.0)
        half = 0.5 * live_ref[pl.ds(s, 1), :].astype(jnp.float32)
        sw[side, s] = half * count * (1.0 - 2.0 * hot)


def kernel(
    scale, panel, slots, nneg,
    emb_ref, cls_ref, valid_ref, short_ref, live_ref, pos_ref, neg_ref,
    wg_ref, eg_ref,
    G, emb2, embh, sw, dl, K, eg, eg_in, short_in, live_in, pos_in, neg_in,
    a1_out, a1_in, b1_out, b1_in, sum_a, sum_b, a2_out, a2_in, b2_out, b2_in,
    V, z_out, z_in, part,
    send, recv,
):
    at = Place()
    docs, width = emb_ref.shape
    right, left, up, down = at.along_x(1), at.along_x(-1), at.along_y(1), at.along_y(-1)
    sibling = at.sibling()
    barrier = pltpu.get_barrier_semaphore()
    partners = [right, left, up, down, sibling]
    partners += [at.along_enc(k) for k in range(1, 4)] + [at.across(k) for k in range(4)]
    for device in partners:
        pl.semaphore_signal(barrier, inc=1, device_id=device, device_id_type=MESH)

    rows = lax.broadcasted_iota(jnp.int32, (panel, panel), 0)
    cols = lax.broadcasted_iota(jnp.int32, (panel, panel), 1)
    flags = jnp.where(rows == cols, valid_ref[...].astype(jnp.float32), 0.0)
    valid = jnp.sum(flags, axis=1, keepdims=True)
    mine = (cls_ref[...] * valid).astype(jnp.bfloat16)
    G[0, 0, 0] = mine.reshape(2, 2, 16, width)
    pl.semaphore_wait(barrier, len(partners))

    mail = Mail(send, recv)

    def score(rh, parts):
        w = [G[rh, :, f, 0] if k == 0 else G[rh, f, :, 1] for k, f in parts]
        w = jnp.concatenate([block.reshape(2 * panel, width) for block in w], axis=0)
        labels = w.shape[0]
        half_logits = lax.dot_general(w, embh[...], NT, preferred_element_type=jnp.float32)
        h = at.h if rh == 0 else 1 - at.h
        row = 0
        for k, f in parts:
            for t in range(4):
                ry, rx = (t, f) if k == 0 else (f, t)
                cluster = at.lab_of(h, rem4(at.y + ry), rem4(at.x + rx), at.c)
                for side, short in enumerate((short_ref, short_in)):
                    hw = None
                    for s in range(slots):
                        term = sw[side, s, pl.ds(k * panel // 2, panel // 2)] * jnp.where(
                            short[pl.ds(s, 1), :] == cluster, 1.0, 0.0
                        )
                        hw = term if hw is None else hw + term
                    t = jnp.tanh(half_logits[row : row + panel // 2, side * docs : (side + 1) * docs])
                    dl[pl.ds(row, panel // 2), pl.ds(side * docs, docs)] = (jnp.abs(hw) * t + hw).astype(jnp.bfloat16)
                row += panel // 2
        d = dl[pl.ds(0, labels), :]
        grad = jnp.dot(d, emb2[...], preferred_element_type=jnp.float32)
        for n, (k, f) in enumerate(parts):
            part_grad = grad[n * 2 * panel : (n + 1) * 2 * panel].reshape(4, 2, 16, width)
            if k == 0:
                K[rh, :, f, 0] = part_grad
            else:
                K[rh, f, :, 1] = part_grad
        eg[...] += lax.dot_general(d, w, TN, preferred_element_type=jnp.float32)

    def term_a(rh):
        return lambda g, rel, s: K[rh, g, rel, 0, s]

    def term_b(rh):
        return lambda g, rel, s: K[rh, rel, g, 1, s]

    def ring(out, into, rh, groups, value, plus, minus):
        return RingSum(mail, out, into, rh, groups, value, plus, minus)

    a1 = [ring(a1_out, a1_in, rh, 4, term_a(rh), right, left) for rh in (0, 1)]
    b1 = [ring(b1_out, b1_in, rh, 4, term_b(rh), up, down) for rh in (0, 1)]
    a2 = [ring(a2_out, a2_in, rh, 1, lambda g, rel, s, rh=rh: sum_a[rh, rel, s], up, down) for rh in (0, 1)]
    b2 = [ring(b2_out, b2_in, rh, 1, lambda g, rel, s, rh=rh: sum_b[rh, rel, s], right, left) for rh in (0, 1)]

    def first_far(rh):
        a1[rh].far()
        b1[rh].far()

    def first_near(rh):
        for way in (0, 1):
            a1[rh].near(way)
            b1[rh].near(way)

    def first_relays(rh):
        for way in (0, 1):
            a1[rh].relay(way)
            b1[rh].relay(way)

    def second_sends(rh):
        def store_a(g, s, v):
            sum_a[rh, g, s] = v

        def store_b(g, s, v):
            sum_b[rh, g, s] = v

        a1[rh].collect(store_a)
        a2[rh].far()
        b1[rh].collect(store_b)
        b2[rh].far()
        for way in (0, 1):
            a2[rh].near(way)
            b2[rh].near(way)

    def second_relays(rh):
        for way in (0, 1):
            a2[rh].relay(way)
            b2[rh].relay(way)

    def plane_sum(rh):
        def store(half):
            def put(g, s, v):
                V[rh, 2 * half + s] = v
                z_out[rh, 2 * half + s] = v.astype(jnp.bfloat16)

            return put

        a2[rh].collect(store(0))
        b2[rh].collect(store(1))

    slices = []

    def z_sends(rh):
        for k in range(1 - rh, 4):
            device = at.across(k) if rh else at.along_enc(k)
            slices.append(mail.post((z_out, rh, rem4(at.e + k)), (z_in, len(slices)), device))

    posted = {}
    devices = (right, left, up, down)
    mirror = at.mirror()

    def piece(key):
        rh, k, s, ry, rx = key
        return (G, rh, ry, rx, k) if s is None else (G, rh, ry, rx, k, s)

    def follow(plan):
        for what in plan:
            if what[0] == "chunk":
                score(*what[1:])
            elif what[0] == "send":
                src = what[1] if what[2][2] is None else what[1][:2] + what[2][2:3] + what[1][3:]
                posted[what[2]] = mail.post(piece(src), piece(what[2]), devices[what[3]])
            elif what[1] in posted:
                posted[what[1]].wait_recv()

    plan = gather_plan([(0, ((k, f), (k, f + 1))) for f in (2, 0) for k in (0, 1)])
    opening = next(n for n, what in enumerate(plan) if what[0] == "wait" and (what[1][0] or what[1][3] or what[1][4]))
    follow(plan[:opening])
    for k in (0, 1):
        posted[1, k, None, 0, 0] = mail.post((G, 0, 0, 0, k), (G, 1, 0, 0, k), mirror)
    whole = slice(None)
    shared = [
        mail.post((src, whole), (dst, whole), sibling)
        for src, dst in ((short_ref, short_in), (live_ref, live_in), (pos_ref, pos_in), (neg_ref, neg_in))
    ]
    shared.append(mail.post((emb_ref, whole), (emb2, pl.ds(docs, docs)), sibling))
    emb2[pl.ds(0, docs), :] = emb_ref[...]
    embh[pl.ds(0, docs), :] = emb_ref[...] * jnp.bfloat16(0.5)
    slot_weights(live_ref, pos_ref, neg_ref, sw, 0, panel, slots, nneg)
    eg[...] = jnp.zeros_like(eg)
    for copy in shared:
        copy.wait_recv()
    slot_weights(live_in, pos_in, neg_in, sw, 1, panel, slots, nneg)
    embh[pl.ds(docs, docs), :] = emb2[pl.ds(docs, docs), :] * jnp.bfloat16(0.5)
    follow(plan[opening:])
    first_far(0)
    first_near(0)
    score(1, ((0, 2), (1, 2)))
    first_relays(0)
    first_far(1)
    score(1, ((0, 1), (0, 3), (1, 1), (1, 3)))
    first_near(1)
    first_relays(1)
    score(1, ((0, 0), (1, 0)))
    returned = mail.post((eg, pl.ds(docs, docs)), (eg_in, whole), sibling)
    second_sends(0)
    second_relays(0)
    second_sends(1)
    plane_sum(0)
    z_sends(0)
    returned.wait_recv()
    eg_ref[...] = eg[pl.ds(0, docs), :] + eg_in[...]
    second_relays(1)
    plane_sum(1)
    z_sends(1)

    total = V[0, at.e]
    for k, copy in enumerate(slices):
        copy.wait_recv()
        total += z_in[k].astype(jnp.float32)
    part[at.e] = total * scale
    shares = [mail.post((part, at.e), (part, at.e), at.along_enc(k)) for k in range(1, 4)]
    for copy in shares:
        copy.wait_recv()
    wg_ref[...] = part[...].reshape(panel, width) * valid

    mail.finish()


def shards(embeddings, classifier, label_valid, shortlist, slot_live, positive, negative):
    lab_count = lax.axis_size("lab")
    enc_count = lax.axis_size("enc")
    docs, width = embeddings.shape
    panel = classifier.shape[0]
    slots = shortlist.shape[1]
    nneg = negative.shape[2]
    scale = 1.0 / math.sqrt(docs * enc_count * slots)
    by_slot = lambda a: a.transpose(1, 0)
    vmem = pl.BlockSpec(memory_space=pltpu.VMEM)
    bf16, f32 = jnp.bfloat16, jnp.float32
    piece = (16, width)
    return pl.pallas_call(
        functools.partial(kernel, scale, panel, slots, nneg),
        out_shape=(pltpu.VMEM((panel, width), f32), pltpu.VMEM((docs, width), f32)),
        in_specs=[vmem] * 7,
        out_specs=(vmem, vmem),
        scratch_shapes=[
            pltpu.VMEM((2, 4, 4, 2, 2) + piece, bf16),
            pltpu.VMEM((2 * docs, width), bf16),
            pltpu.VMEM((2 * docs, width), bf16),
            pltpu.VMEM((2, slots, panel, docs), f32),
            pltpu.VMEM((8 * panel, 2 * docs), bf16),
            pltpu.VMEM((2, 4, 4, 2, 2) + piece, f32),
            pltpu.VMEM((2 * docs, width), f32),
            pltpu.VMEM((docs, width), f32),
            pltpu.VMEM((slots, docs), jnp.int32),
            pltpu.VMEM((slots, docs), jnp.int32),
            pltpu.VMEM((slots, docs), jnp.int32),
            pltpu.VMEM((slots * nneg, docs), jnp.int32),
            pltpu.VMEM((2, 2, 3, 4) + piece, bf16),
            pltpu.VMEM((2, 2, 3, 4) + piece, bf16),
            pltpu.VMEM((2, 2, 3, 4) + piece, bf16),
            pltpu.VMEM((2, 2, 3, 4) + piece, bf16),
            pltpu.VMEM((2, 4, 2) + piece, f32),
            pltpu.VMEM((2, 4, 2) + piece, f32),
            pltpu.VMEM((2, 2, 3, 1) + piece, bf16),
            pltpu.VMEM((2, 2, 3, 1) + piece, bf16),
            pltpu.VMEM((2, 2, 3, 1) + piece, bf16),
            pltpu.VMEM((2, 2, 3, 1) + piece, bf16),
            pltpu.VMEM((2, 4) + piece, f32),
            pltpu.VMEM((2, 4) + piece, bf16),
            pltpu.VMEM((7,) + piece, bf16),
            pltpu.VMEM((4,) + piece, f32),
            pltpu.SemaphoreType.DMA((192,)),
            pltpu.SemaphoreType.DMA((192,)),
        ],
        compiler_params=pltpu.CompilerParams(
            collective_id=0, has_side_effects=True, vmem_limit_bytes=60 * 1024 * 1024
        ),
        name="step",
    )(
        embeddings,
        classifier,
        label_valid.reshape(1, panel),
        by_slot(shortlist),
        by_slot(slot_live),
        by_slot(positive),
        negative.transpose(1, 2, 0).reshape(slots * nneg, docs),
    )


def solution(mesh):
    in_specs = (
        P(("enc", "lab"), None),
        P("lab", None),
        P("lab"),
        P(("enc", "lab"), None),
        P(("enc", "lab"), None),
        P(("enc", "lab"), None),
        P(("enc", "lab"), None, None),
    )
    out_specs = (P("lab", None), P(("enc", "lab"), None))
    return jax.shard_map(shards, mesh=mesh, in_specs=in_specs, out_specs=out_specs, check_vma=False)
```

```python
import functools
import heapq
import math

import jax
import jax.numpy as jnp
from jax import lax
from jax.experimental import pallas as pl
from jax.experimental.pallas import tpu as pltpu
from jax.sharding import PartitionSpec as P

MESH = pl.DeviceIdType.MESH
NT = (((1,), (1,)), ((), ()))
TN = (((0,), (0,)), ((), ()))


def rem4(v):
    return lax.rem(v + 8, 4)


class Place:
    def __init__(self):
        self.e = lax.axis_index("enc")
        lab = lax.axis_index("lab")
        self.c = lax.rem(lab, 2)
        self.x = lax.rem(lax.div(lab, 2), 4)
        self.y = lax.rem(lax.div(lab, 8), 4)
        self.h = lax.div(lab, 32)

    def lab_of(self, h, y, x, c):
        return ((h * 4 + y) * 4 + x) * 2 + c

    def along_x(self, k):
        return (self.e, self.lab_of(self.h, self.y, rem4(self.x + k), self.c))

    def along_y(self, k):
        return (self.e, self.lab_of(self.h, rem4(self.y + k), self.x, self.c))

    def sibling(self):
        return (self.e, self.lab_of(self.h, self.y, self.x, 1 - self.c))

    def mirror(self):
        return (3 - self.e, self.lab_of(1 - self.h, self.y, self.x, self.c))

    def across(self, k):
        return (rem4(self.e + k), self.lab_of(1 - self.h, self.y, self.x, self.c))

    def along_enc(self, k):
        return (rem4(self.e + k), self.lab_of(self.h, self.y, self.x, self.c))


class Copy:
    def __init__(self, mail, n, src, dst, device):
        self.mail, self.n, self.src, self.dst, self.device = mail, n, src, dst, device

    def made(self):
        return pltpu.make_async_remote_copy(
            src_ref=self.src[0].at[self.src[1:]],
            dst_ref=self.dst[0].at[self.dst[1:]],
            send_sem=self.mail.send.at[self.n],
            recv_sem=self.mail.recv.at[self.n],
            device_id=self.device,
            device_id_type=MESH,
        )

    def wait_recv(self):
        self.made().wait_recv()


class Mail:
    def __init__(self, send, recv):
        self.send, self.recv, self.sent = send, recv, []

    def post(self, src, dst, device):
        copy = Copy(self, len(self.sent), src, dst, device)
        copy.made().start()
        self.sent.append(copy)
        return copy

    def finish(self):
        for copy in self.sent:
            copy.made().wait_send()


RIGHT, LEFT, UP, DOWN = range(4)


def onward(key):
    rh, k, s, ry, rx = key
    first, second = (rx, ry) if k == 0 else (ry, rx)
    ways = ((RIGHT, LEFT), (UP, DOWN)) if k == 0 else ((UP, DOWN), (RIGHT, LEFT))

    def there(s, f, t):
        return (rh, k, s, t, f) if k == 0 else (rh, k, s, f, t)

    out = []
    if second == 0:
        if first == 0:
            out += [(ways[0][0], there(None, 3, 0), 4), (ways[0][1], there(None, 1, 0), 4)]
        elif first != 2:
            s = 0 if first == 3 else 1
            out += [(ways[0][s], there(s, 2, 0), 3)]
        out += [(ways[1][0], there(None, first, 3), 2), (ways[1][1], there(None, first, 1), 2)]
    elif second != 2:
        s = 0 if second == 3 else 1
        out += [(ways[1][s], there(s, first, 2), 1)]
    return out


def gather_plan(chunks, rings, wire=0.6, hop=2.6, chunk_time=0.95):
    plan, free, now = [], [0.0] * 4, 0.0
    events = [(0.0, k, (0, k, None, 0, 0)) for k in (0, 1)] + [(5.0 + 2.0 * k, 2 + k, (1, k, None, 0, 0)) for k in (0, 1)]
    heapq.heapify(events)
    order, have, todo, rings = 4, set(), list(chunks), list(rings)

    def runnable():
        for rh, parts in todo:
            places = [(k, t, f) if k == 0 else (k, f, t) for k, f in parts for t in range(4)]
            if all((rh,) + place in have for place in places):
                return rh, parts
        return None

    while events or todo:
        chunk = runnable()
        quiet = not events or events[0][0] > now + 0.5 or min(free) > now + 1.5
        if chunk and quiet:
            todo.remove(chunk)
            plan.append(("chunk",) + chunk)
            now += chunk_time * len(chunk[1])
            continue
        for ring in list(rings):
            needs, way, message = ring
            if not any(rest in needs for rest in todo) and free[way] < now + 0.3:
                rings.remove(ring)
                plan.append(("ring",) + message)
                free[way] = max(now, free[way]) + 8 * wire / 2
                now += 0.1
        if not events:
            now += 0.5
            continue
        now = max(now, events[0][0])
        sends = []
        while events and events[0][0] <= now:
            key = heapq.heappop(events)[2]
            plan.append(("wait", key))
            now += 0.03
            rh, k, s, ry, rx = key
            if s is not None:
                if (rh, k, 1 - s, ry, rx) not in have:
                    have.add(key)
                    continue
                key = (rh, k, None, ry, rx)
            have.add((rh, k, ry, rx))
            sends += [(-left, rh, way, key, then) for way, then, left in onward(key)]
        for _, _, way, key, then in sorted(sends, key=lambda send: send[:3]):
            free[way] = max(now, free[way]) + (wire if then[2] is not None else 2 * wire)
            heapq.heappush(events, (free[way] + hop, order, then))
            order += 1
            now += 0.03
            plan.append(("send", key, then, way))
    return plan + [("ring",) + message for _, _, message in rings]


class RingSum:
    def __init__(self, mail, out, into, rh, groups, value, plus, minus):
        self.mail, self.out, self.into, self.rh, self.groups, self.value = mail, out, into, rh, groups, value
        self.plus, self.minus = plus, minus
        self.copies = {}

    def fill(self, way, slot, make):
        def one(g, carry):
            self.out[self.rh, way, slot, g] = make(g).astype(jnp.bfloat16)
            return carry

        lax.fori_loop(0, self.groups, one, 0, unroll=True)
        self.copies[way, slot] = self.mail.post(
            (self.out, self.rh, way, slot), (self.into, self.rh, way, slot), self.minus if way else self.plus
        )

    def far(self, way):
        self.fill(way, 0, lambda g: self.value(g, 2, way))

    def near(self, way):
        self.fill(way, 1, lambda g: self.value(g, 3 if way else 1, 0 if way else 1))

    def got(self, way, slot, g):
        return self.into[self.rh, way, slot, g].astype(jnp.float32)

    def relay(self, way):
        self.copies[way, 0].wait_recv()
        self.fill(way, 2, lambda g: self.value(g, 3 if way else 1, way) + self.got(way, 0, g))

    def collect(self, store):
        for way in (0, 1):
            for slot in (1, 2):
                self.copies[way, slot].wait_recv()

        def one(g, carry):
            store(g, 0, self.value(g, 0, 0) + self.got(0, 2, g) + self.got(1, 1, g))
            store(g, 1, self.value(g, 0, 1) + self.got(0, 1, g) + self.got(1, 2, g))
            return carry

        lax.fori_loop(0, self.groups, one, 0, unroll=True)


def slot_weights(live_ref, pos_ref, neg_ref, sw, side, panel, slots, nneg):
    docs = pos_ref.shape[1]
    label = lax.broadcasted_iota(jnp.int32, (panel, docs), 0)
    for s in range(slots):
        hot = jnp.where(pos_ref[pl.ds(s, 1), :] == label, 1.0, 0.0)
        count = hot
        for k in range(nneg):
            count += jnp.where(neg_ref[pl.ds(s * nneg + k, 1), :] == label, 1.0, 0.0)
        half = 0.5 * live_ref[pl.ds(s, 1), :].astype(jnp.float32)
        sw[side, s] = half * count * (1.0 - 2.0 * hot)


def kernel(
    scale, panel, slots, nneg,
    emb_hbm, cls_ref, valid_ref, short_hbm, live_hbm, pos_hbm, neg_hbm,
    wg_ref, eg_ref,
    G, emb2, embh, sw, dl, K, eg, eg_in, short_ref, live_ref, pos_ref, neg_ref, short_in, live_in, pos_in, neg_in,
    a1_out, a1_in, b1_out, b1_in, sum_a, sum_b, a2_out, a2_in, b2_out, b2_in,
    V, z_out, z_in, part,
    send, recv, fetch,
):
    at = Place()
    docs, width = emb_hbm.shape
    right, left, up, down = at.along_x(1), at.along_x(-1), at.along_y(1), at.along_y(-1)
    sibling = at.sibling()
    barrier = pltpu.get_barrier_semaphore()
    partners = [right, left, up, down, sibling]
    partners += [at.along_enc(k) for k in range(1, 4)] + [at.across(k) for k in range(4)]
    for device in partners:
        pl.semaphore_signal(barrier, inc=1, device_id=device, device_id_type=MESH)

    emb_ref = emb2.at[pl.ds(0, docs)]
    fetched = [
        pltpu.make_async_copy(src, dst, fetch.at[n])
        for n, (src, dst) in enumerate(
            (
                (short_hbm, short_ref),
                (live_hbm, live_ref),
                (pos_hbm, pos_ref),
                (neg_hbm, neg_ref),
                (emb_hbm, emb_ref),
            )
        )
    ]
    for copy in fetched:
        copy.start()

    rows = lax.broadcasted_iota(jnp.int32, (panel, panel), 0)
    cols = lax.broadcasted_iota(jnp.int32, (panel, panel), 1)
    flags = jnp.where(rows == cols, valid_ref[...].astype(jnp.float32), 0.0)
    valid = jnp.sum(flags, axis=1, keepdims=True)
    mine = (cls_ref[...] * valid).astype(jnp.bfloat16)
    G[0, 0, 0] = mine.reshape(2, 2, 16, width)
    pl.semaphore_wait(barrier, len(partners))

    mail = Mail(send, recv)

    def score(rh, parts):
        w = [G[rh, :, f, 0] if k == 0 else G[rh, f, :, 1] for k, f in parts]
        w = jnp.concatenate([block.reshape(2 * panel, width) for block in w], axis=0)
        labels = w.shape[0]
        half_logits = lax.dot_general(w, embh[...], NT, preferred_element_type=jnp.float32)
        h = at.h if rh == 0 else 1 - at.h
        row = 0
        for k, f in parts:
            for t in range(4):
                ry, rx = (t, f) if k == 0 else (f, t)
                cluster = at.lab_of(h, rem4(at.y + ry), rem4(at.x + rx), at.c)
                for side, short in enumerate((short_ref, short_in)):
                    hw = None
                    for s in range(slots):
                        term = sw[side, s, pl.ds(k * panel // 2, panel // 2)] * jnp.where(
                            short[pl.ds(s, 1), :] == cluster, 1.0, 0.0
                        )
                        hw = term if hw is None else hw + term
                    t = jnp.tanh(half_logits[row : row + panel // 2, side * docs : (side + 1) * docs])
                    dl[pl.ds(row, panel // 2), pl.ds(side * docs, docs)] = (jnp.abs(hw) * t + hw).astype(jnp.bfloat16)
                row += panel // 2
        d = dl[pl.ds(0, labels), :]
        grad = jnp.dot(d, emb2[...], preferred_element_type=jnp.float32)
        for n, (k, f) in enumerate(parts):
            part_grad = grad[n * 2 * panel : (n + 1) * 2 * panel].reshape(4, 2, 16, width)
            if k == 0:
                K[rh, :, f, 0] = part_grad
            else:
                K[rh, f, :, 1] = part_grad
        eg[...] += lax.dot_general(d, w, TN, preferred_element_type=jnp.float32)

    def term_a(rh):
        return lambda g, rel, s: K[rh, g, rel, 0, s]

    def term_b(rh):
        return lambda g, rel, s: K[rh, rel, g, 1, s]

    def ring(out, into, rh, groups, value, plus, minus):
        return RingSum(mail, out, into, rh, groups, value, plus, minus)

    a1 = [ring(a1_out, a1_in, rh, 4, term_a(rh), right, left) for rh in (0, 1)]
    b1 = [ring(b1_out, b1_in, rh, 4, term_b(rh), up, down) for rh in (0, 1)]
    a2 = [ring(a2_out, a2_in, rh, 1, lambda g, rel, s, rh=rh: sum_a[rh, rel, s], up, down) for rh in (0, 1)]
    b2 = [ring(b2_out, b2_in, rh, 1, lambda g, rel, s, rh=rh: sum_b[rh, rel, s], right, left) for rh in (0, 1)]

    def first_far(rh):
        for way in (0, 1):
            a1[rh].far(way)
            b1[rh].far(way)

    def first_relays(rh):
        for way in (0, 1):
            a1[rh].relay(way)
            b1[rh].relay(way)

    def second_sends(rh):
        def store_a(g, s, v):
            sum_a[rh, g, s] = v

        def store_b(g, s, v):
            sum_b[rh, g, s] = v

        a1[rh].collect(store_a)
        for way in (0, 1):
            a2[rh].far(way)
        b1[rh].collect(store_b)
        for way in (0, 1):
            b2[rh].far(way)
        for way in (0, 1):
            a2[rh].near(way)
            b2[rh].near(way)

    def second_relays(rh):
        for way in (0, 1):
            a2[rh].relay(way)
            b2[rh].relay(way)

    def plane_sum(rh):
        def store(half):
            def put(g, s, v):
                V[rh, 2 * half + s] = v
                z_out[rh, 2 * half + s] = v.astype(jnp.bfloat16)

            return put

        a2[rh].collect(store(0))
        b2[rh].collect(store(1))

    slices = []

    def z_sends(rh):
        for k in range(1 - rh, 4):
            device = at.across(k) if rh else at.along_enc(k)
            slices.append(mail.post((z_out, rh, rem4(at.e + k)), (z_in, len(slices)), device))

    posted = {}
    devices = (right, left, up, down)
    mirror = at.mirror()

    def piece(key):
        rh, k, s, ry, rx = key
        return (G, rh, ry, rx, k) if s is None else (G, rh, ry, rx, k, s)

    def follow(plan):
        for what in plan:
            if what[0] == "chunk":
                score(*what[1:])
            elif what[0] == "ring":
                rh, of_b, distance, way = what[1:]
                ring = (b1 if of_b else a1)[rh]
                if distance == 2:
                    ring.far(way)
                else:
                    ring.near(way)
            elif what[0] == "send":
                src = what[1] if what[2][2] is None else what[1][:2] + what[2][2:3] + what[1][3:]
                posted[what[2]] = mail.post(piece(src), piece(what[2]), devices[what[3]])
            elif what[1] in posted:
                posted[what[1]].wait_recv()

    first_half = [(0, ((k, f), (k, f + 1))) for f in (2, 0) for k in (0, 1)]
    own_place, beside = (1, ((0, 0), (1, 0))), (1, ((0, 1), (0, 3), (1, 1), (1, 3)))
    rings = [(first_half, 2 * b + way, (0, b, d, way)) for d in (2, 1) for b in (0, 1) for way in (0, 1)]
    rings += [([beside], 2 * b + way, (1, b, 1, way)) for b in (0, 1) for way in (0, 1)]
    plan = gather_plan(first_half + [own_place, beside], rings)
    opening = next(n for n, what in enumerate(plan) if what[0] == "wait" and (what[1][0] or what[1][3] or what[1][4]))
    follow(plan[:opening])
    for k in (0, 1):
        posted[1, k, None, 0, 0] = mail.post((G, 0, 0, 0, k), (G, 1, 0, 0, k), mirror)
    whole = slice(None)
    for copy in fetched:
        copy.wait()
    shared = [
        mail.post((src, whole), (dst, whole), sibling)
        for src, dst in ((short_ref, short_in), (live_ref, live_in), (pos_ref, pos_in), (neg_ref, neg_in))
    ]
    shared.append(mail.post((emb2, pl.ds(0, docs)), (emb2, pl.ds(docs, docs)), sibling))
    embh[pl.ds(0, docs), :] = emb2[pl.ds(0, docs), :] * jnp.bfloat16(0.5)
    slot_weights(live_ref, pos_ref, neg_ref, sw, 0, panel, slots, nneg)
    eg[...] = jnp.zeros_like(eg)
    for copy in shared:
        copy.wait_recv()
    slot_weights(live_in, pos_in, neg_in, sw, 1, panel, slots, nneg)
    embh[pl.ds(docs, docs), :] = emb2[pl.ds(docs, docs), :] * jnp.bfloat16(0.5)
    follow(plan[opening:])
    score(1, ((0, 2), (1, 2)))
    first_far(1)
    returned = mail.post((eg, pl.ds(docs, docs)), (eg_in, whole), sibling)
    first_relays(0)
    first_relays(1)
    second_sends(0)
    second_relays(0)
    second_sends(1)
    plane_sum(0)
    z_sends(0)
    returned.wait_recv()
    eg_ref[...] = eg[pl.ds(0, docs), :] + eg_in[...]
    second_relays(1)
    plane_sum(1)
    z_sends(1)

    total = V[0, at.e]
    for k, copy in enumerate(slices):
        copy.wait_recv()
        total += z_in[k].astype(jnp.float32)
    part[at.e] = total * scale
    shares = [mail.post((part, at.e), (part, at.e), at.along_enc(k)) for k in range(1, 4)]
    for copy in shares:
        copy.wait_recv()
    wg_ref[...] = part[...].reshape(panel, width) * valid

    mail.finish()


def shards(embeddings, classifier, label_valid, shortlist, slot_live, positive, negative):
    lab_count = lax.axis_size("lab")
    enc_count = lax.axis_size("enc")
    docs, width = embeddings.shape
    panel = classifier.shape[0]
    slots = shortlist.shape[1]
    nneg = negative.shape[2]
    scale = 1.0 / math.sqrt(docs * enc_count * slots)
    by_slot = lambda a: a.transpose(1, 0)
    vmem, hbm = pl.BlockSpec(memory_space=pltpu.VMEM), pl.BlockSpec(memory_space=pl.ANY)
    bf16, f32 = jnp.bfloat16, jnp.float32
    piece = (16, width)
    return pl.pallas_call(
        functools.partial(kernel, scale, panel, slots, nneg),
        out_shape=(pltpu.VMEM((panel, width), f32), pltpu.VMEM((docs, width), f32)),
        in_specs=[hbm, vmem, vmem] + [hbm] * 4,
        out_specs=(vmem, vmem),
        scratch_shapes=[
            pltpu.VMEM((2, 4, 4, 2, 2) + piece, bf16),
            pltpu.VMEM((2 * docs, width), bf16),
            pltpu.VMEM((2 * docs, width), bf16),
            pltpu.VMEM((2, slots, panel, docs), f32),
            pltpu.VMEM((8 * panel, 2 * docs), bf16),
            pltpu.VMEM((2, 4, 4, 2, 2) + piece, f32),
            pltpu.VMEM((2 * docs, width), f32),
            pltpu.VMEM((docs, width), f32),
            pltpu.VMEM((slots, docs), jnp.int32),
            pltpu.VMEM((slots, docs), jnp.int32),
            pltpu.VMEM((slots, docs), jnp.int32),
            pltpu.VMEM((slots * nneg, docs), jnp.int32),
            pltpu.VMEM((slots, docs), jnp.int32),
            pltpu.VMEM((slots, docs), jnp.int32),
            pltpu.VMEM((slots, docs), jnp.int32),
            pltpu.VMEM((slots * nneg, docs), jnp.int32),
            pltpu.VMEM((2, 2, 3, 4) + piece, bf16),
            pltpu.VMEM((2, 2, 3, 4) + piece, bf16),
            pltpu.VMEM((2, 2, 3, 4) + piece, bf16),
            pltpu.VMEM((2, 2, 3, 4) + piece, bf16),
            pltpu.VMEM((2, 4, 2) + piece, f32),
            pltpu.VMEM((2, 4, 2) + piece, f32),
            pltpu.VMEM((2, 2, 3, 1) + piece, bf16),
            pltpu.VMEM((2, 2, 3, 1) + piece, bf16),
            pltpu.VMEM((2, 2, 3, 1) + piece, bf16),
            pltpu.VMEM((2, 2, 3, 1) + piece, bf16),
            pltpu.VMEM((2, 4) + piece, f32),
            pltpu.VMEM((2, 4) + piece, bf16),
            pltpu.VMEM((7,) + piece, bf16),
            pltpu.VMEM((4,) + piece, f32),
            pltpu.SemaphoreType.DMA((192,)),
            pltpu.SemaphoreType.DMA((192,)),
            pltpu.SemaphoreType.DMA((5,)),
        ],
        compiler_params=pltpu.CompilerParams(
            collective_id=0, has_side_effects=True, vmem_limit_bytes=60 * 1024 * 1024
        ),
        name="step",
    )(
        embeddings,
        classifier,
        label_valid.reshape(1, panel),
        by_slot(shortlist),
        by_slot(slot_live),
        by_slot(positive),
        negative.transpose(1, 2, 0).reshape(slots * nneg, docs),
    )


def solution(mesh):
    in_specs = (
        P(("enc", "lab"), None),
        P("lab", None),
        P("lab"),
        P(("enc", "lab"), None),
        P(("enc", "lab"), None),
        P(("enc", "lab"), None),
        P(("enc", "lab"), None, None),
    )
    out_specs = (P("lab", None), P(("enc", "lab"), None))
    return jax.shard_map(shards, mesh=mesh, in_specs=in_specs, out_specs=out_specs, check_vma=False)
```

```python
import functools
import heapq
import math

import jax
import jax.numpy as jnp
from jax import lax
from jax.experimental import pallas as pl
from jax.experimental.pallas import tpu as pltpu
from jax.sharding import PartitionSpec as P

MESH = pl.DeviceIdType.MESH
NT = (((1,), (1,)), ((), ()))
TN = (((0,), (0,)), ((), ()))


def rem4(v):
    return lax.rem(v + 8, 4)


class Place:
    def __init__(self):
        self.e = lax.axis_index("enc")
        lab = lax.axis_index("lab")
        self.c = lax.rem(lab, 2)
        self.x = lax.rem(lax.div(lab, 2), 4)
        self.y = lax.rem(lax.div(lab, 8), 4)
        self.h = lax.div(lab, 32)

    def lab_of(self, h, y, x, c):
        return ((h * 4 + y) * 4 + x) * 2 + c

    def along_x(self, k):
        return (self.e, self.lab_of(self.h, self.y, rem4(self.x + k), self.c))

    def along_y(self, k):
        return (self.e, self.lab_of(self.h, rem4(self.y + k), self.x, self.c))

    def sibling(self):
        return (self.e, self.lab_of(self.h, self.y, self.x, 1 - self.c))

    def mirror(self):
        return (3 - self.e, self.lab_of(1 - self.h, self.y, self.x, self.c))

    def across(self, k):
        return (rem4(self.e + k), self.lab_of(1 - self.h, self.y, self.x, self.c))

    def along_enc(self, k):
        return (rem4(self.e + k), self.lab_of(self.h, self.y, self.x, self.c))


class Copy:
    def __init__(self, mail, n, src, dst, device):
        self.mail, self.n, self.src, self.dst, self.device = mail, n, src, dst, device

    def made(self):
        return pltpu.make_async_remote_copy(
            src_ref=self.src[0].at[self.src[1:]],
            dst_ref=self.dst[0].at[self.dst[1:]],
            send_sem=self.mail.send.at[self.n],
            recv_sem=self.mail.recv.at[self.n],
            device_id=self.device,
            device_id_type=MESH,
        )

    def wait_recv(self):
        self.made().wait_recv()


class Mail:
    def __init__(self, send, recv):
        self.send, self.recv, self.sent = send, recv, []

    def post(self, src, dst, device):
        copy = Copy(self, len(self.sent), src, dst, device)
        copy.made().start()
        self.sent.append(copy)
        return copy

    def finish(self):
        for copy in self.sent:
            copy.made().wait_send()


RIGHT, LEFT, UP, DOWN = range(4)


def onward(key):
    rh, k, s, ry, rx = key
    first, second = (rx, ry) if k == 0 else (ry, rx)
    ways = ((RIGHT, LEFT), (UP, DOWN)) if k == 0 else ((UP, DOWN), (RIGHT, LEFT))

    def there(s, f, t):
        return (rh, k, s, t, f) if k == 0 else (rh, k, s, f, t)

    out = []
    if second == 0:
        if first == 0:
            out += [(ways[0][0], there(None, 3, 0), 4), (ways[0][1], there(None, 1, 0), 4)]
        elif first != 2:
            s = 0 if first == 3 else 1
            out += [(ways[0][s], there(s, 2, 0), 3)]
        out += [(ways[1][0], there(None, first, 3), 2), (ways[1][1], there(None, first, 1), 2)]
    elif second != 2:
        s = 0 if second == 3 else 1
        out += [(ways[1][s], there(s, first, 2), 1)]
    return out


def gather_plan(chunks, rings, wire=0.6, hop=2.6, chunk_time=0.95):
    plan, free, now = [], [0.0] * 4, 0.0
    events = [(0.0, k, (0, k, None, 0, 0)) for k in (0, 1)] + [(5.0 + 2.0 * k, 2 + k, (1, k, None, 0, 0)) for k in (0, 1)]
    heapq.heapify(events)
    order, have, todo, rings, first_ring = 4, set(), list(chunks), list(rings), 1e9

    def runnable():
        for rh, parts in todo:
            places = [(k, t, f) if k == 0 else (k, f, t) for k, f in parts for t in range(4)]
            if all((rh,) + place in have for place in places):
                return rh, parts
        return None

    while events or todo:
        chunk = runnable()
        quiet = not events or events[0][0] > now + 0.5 or min(free) > now + 1.5
        if chunk and quiet:
            todo.remove(chunk)
            plan.append(("chunk",) + chunk)
            now += chunk_time * len(chunk[1])
            continue
        for ring in list(rings):
            needs, way, message = ring
            if not any(rest in needs for rest in todo) and free[way] < now + 0.3:
                if message[2] == 0 and now < first_ring + 5.5:
                    continue
                first_ring = min(first_ring, now)
                rings.remove(ring)
                plan.append(("ring",) + message)
                free[way] = max(now, free[way]) + 8 * wire / 2
                now += 0.1
        if not events:
            now += 0.5
            continue
        now = max(now, events[0][0])
        sends = []
        while events and events[0][0] <= now:
            key = heapq.heappop(events)[2]
            plan.append(("wait", key))
            now += 0.03
            rh, k, s, ry, rx = key
            if s is not None:
                if (rh, k, 1 - s, ry, rx) not in have:
                    have.add(key)
                    continue
                key = (rh, k, None, ry, rx)
            have.add((rh, k, ry, rx))
            sends += [(-left, rh, way, key, then) for way, then, left in onward(key)]
        for _, _, way, key, then in sorted(sends, key=lambda send: send[:3]):
            free[way] = max(now, free[way]) + (wire if then[2] is not None else 2 * wire)
            heapq.heappush(events, (free[way] + hop, order, then))
            order += 1
            now += 0.03
            plan.append(("send", key, then, way))
    return plan + [("ring",) + message for _, _, message in rings]


class RingSum:
    def __init__(self, mail, out, into, rh, groups, value, plus, minus):
        self.mail, self.out, self.into, self.rh, self.groups, self.value = mail, out, into, rh, groups, value
        self.plus, self.minus = plus, minus
        self.copies = {}

    def fill(self, way, slot, make):
        def one(g, carry):
            self.out[self.rh, way, slot, g] = make(g).astype(jnp.bfloat16)
            return carry

        lax.fori_loop(0, self.groups, one, 0, unroll=True)
        self.copies[way, slot] = self.mail.post(
            (self.out, self.rh, way, slot), (self.into, self.rh, way, slot), self.minus if way else self.plus
        )

    def far(self, way):
        self.fill(way, 0, lambda g: self.value(g, 2, way))

    def near(self, way):
        self.fill(way, 1, lambda g: self.value(g, 3 if way else 1, 0 if way else 1))

    def got(self, way, slot, g):
        return self.into[self.rh, way, slot, g].astype(jnp.float32)

    def relay(self, way):
        self.copies[way, 0].wait_recv()
        self.fill(way, 2, lambda g: self.value(g, 3 if way else 1, way) + self.got(way, 0, g))

    def collect(self, store):
        for way in (0, 1):
            for slot in (1, 2):
                self.copies[way, slot].wait_recv()

        def one(g, carry):
            store(g, 0, self.value(g, 0, 0) + self.got(0, 2, g) + self.got(1, 1, g))
            store(g, 1, self.value(g, 0, 1) + self.got(0, 1, g) + self.got(1, 2, g))
            return carry

        lax.fori_loop(0, self.groups, one, 0, unroll=True)


def slot_weights(live_ref, pos_ref, neg_ref, sw, side, panel, slots, nneg):
    docs = pos_ref.shape[1]
    label = lax.broadcasted_iota(jnp.int32, (panel, docs), 0)
    for s in range(slots):
        hot = jnp.where(pos_ref[pl.ds(s, 1), :] == label, 1.0, 0.0)
        count = hot
        for k in range(nneg):
            count += jnp.where(neg_ref[pl.ds(s * nneg + k, 1), :] == label, 1.0, 0.0)
        half = 0.5 * live_ref[pl.ds(s, 1), :].astype(jnp.float32)
        sw[side, s] = half * count * (1.0 - 2.0 * hot)


def kernel(
    scale, panel, slots, nneg,
    emb_hbm, cls_ref, valid_ref, short_hbm, live_hbm, pos_hbm, neg_hbm,
    wg_ref, eg_ref,
    G, emb2, embh, sw, dl, K, eg, eg_in, short_ref, live_ref, pos_ref, neg_ref, short_in, live_in, pos_in, neg_in,
    a1_out, a1_in, b1_out, b1_in, sum_a, sum_b, a2_out, a2_in, b2_out, b2_in,
    V, z_out, z_in, part,
    send, recv, fetch,
):
    at = Place()
    docs, width = emb_hbm.shape
    right, left, up, down = at.along_x(1), at.along_x(-1), at.along_y(1), at.along_y(-1)
    sibling = at.sibling()
    barrier = pltpu.get_barrier_semaphore()
    partners = [right, left, up, down, sibling]
    partners += [at.along_enc(k) for k in range(1, 4)] + [at.across(k) for k in range(4)]
    for device in partners:
        pl.semaphore_signal(barrier, inc=1, device_id=device, device_id_type=MESH)

    emb_ref = emb2.at[pl.ds(0, docs)]
    fetched = [
        pltpu.make_async_copy(src, dst, fetch.at[n])
        for n, (src, dst) in enumerate(
            (
                (short_hbm, short_ref),
                (live_hbm, live_ref),
                (pos_hbm, pos_ref),
                (neg_hbm, neg_ref),
                (emb_hbm, emb_ref),
            )
        )
    ]
    for copy in fetched:
        copy.start()

    rows = lax.broadcasted_iota(jnp.int32, (panel, panel), 0)
    cols = lax.broadcasted_iota(jnp.int32, (panel, panel), 1)
    flags = jnp.where(rows == cols, valid_ref[...].astype(jnp.float32), 0.0)
    valid = jnp.sum(flags, axis=1, keepdims=True)
    mine = (cls_ref[...] * valid).astype(jnp.bfloat16)
    G[0, 0, 0] = mine.reshape(2, 2, 16, width)
    pl.semaphore_wait(barrier, len(partners))

    mail = Mail(send, recv)

    def score(rh, parts):
        w = [G[rh, :, f, 0] if k == 0 else G[rh, f, :, 1] for k, f in parts]
        w = jnp.concatenate([block.reshape(2 * panel, width) for block in w], axis=0)
        labels = w.shape[0]
        half_logits = lax.dot_general(w, embh[...], NT, preferred_element_type=jnp.float32)
        h = at.h if rh == 0 else 1 - at.h
        row = 0
        for k, f in parts:
            for t in range(4):
                ry, rx = (t, f) if k == 0 else (f, t)
                cluster = at.lab_of(h, rem4(at.y + ry), rem4(at.x + rx), at.c)
                for side, short in enumerate((short_ref, short_in)):
                    hw = None
                    for s in range(slots):
                        term = sw[side, s, pl.ds(k * panel // 2, panel // 2)] * jnp.where(
                            short[pl.ds(s, 1), :] == cluster, 1.0, 0.0
                        )
                        hw = term if hw is None else hw + term
                    t = jnp.tanh(half_logits[row : row + panel // 2, side * docs : (side + 1) * docs])
                    dl[pl.ds(row, panel // 2), pl.ds(side * docs, docs)] = (jnp.abs(hw) * t + hw).astype(jnp.bfloat16)
                row += panel // 2
        d = dl[pl.ds(0, labels), :]
        grad = jnp.dot(d, emb2[...], preferred_element_type=jnp.float32)
        for n, (k, f) in enumerate(parts):
            part_grad = grad[n * 2 * panel : (n + 1) * 2 * panel].reshape(4, 2, 16, width)
            if k == 0:
                K[rh, :, f, 0] = part_grad
            else:
                K[rh, f, :, 1] = part_grad
        eg[...] += lax.dot_general(d, w, TN, preferred_element_type=jnp.float32)

    def term_a(rh):
        return lambda g, rel, s: K[rh, g, rel, 0, s]

    def term_b(rh):
        return lambda g, rel, s: K[rh, rel, g, 1, s]

    def ring(out, into, rh, groups, value, plus, minus):
        return RingSum(mail, out, into, rh, groups, value, plus, minus)

    a1 = [ring(a1_out, a1_in, rh, 4, term_a(rh), right, left) for rh in (0, 1)]
    b1 = [ring(b1_out, b1_in, rh, 4, term_b(rh), up, down) for rh in (0, 1)]
    a2 = [ring(a2_out, a2_in, rh, 1, lambda g, rel, s, rh=rh: sum_a[rh, rel, s], up, down) for rh in (0, 1)]
    b2 = [ring(b2_out, b2_in, rh, 1, lambda g, rel, s, rh=rh: sum_b[rh, rel, s], right, left) for rh in (0, 1)]

    def first_far(rh):
        for way in (0, 1):
            a1[rh].far(way)
            b1[rh].far(way)

    def first_near(rh):
        for way in (0, 1):
            a1[rh].near(way)
            b1[rh].near(way)

    def first_relays(rh):
        for way in (0, 1):
            a1[rh].relay(way)
            b1[rh].relay(way)

    def second_sends(rh):
        def store_a(g, s, v):
            sum_a[rh, g, s] = v

        def store_b(g, s, v):
            sum_b[rh, g, s] = v

        a1[rh].collect(store_a)
        for way in (0, 1):
            a2[rh].far(way)
        b1[rh].collect(store_b)
        for way in (0, 1):
            b2[rh].far(way)
        for way in (0, 1):
            a2[rh].near(way)
            b2[rh].near(way)

    def second_relays(rh):
        for way in (0, 1):
            a2[rh].relay(way)
            b2[rh].relay(way)

    def plane_sum(rh):
        def store(half):
            def put(g, s, v):
                V[rh, 2 * half + s] = v
                z_out[rh, 2 * half + s] = v.astype(jnp.bfloat16)

            return put

        a2[rh].collect(store(0))
        b2[rh].collect(store(1))

    slices = []

    def z_sends(rh):
        for k in range(1 - rh, 4):
            device = at.across(k) if rh else at.along_enc(k)
            slices.append(mail.post((z_out, rh, rem4(at.e + k)), (z_in, len(slices)), device))

    posted = {}
    devices = (right, left, up, down)
    mirror = at.mirror()

    def piece(key):
        rh, k, s, ry, rx = key
        return (G, rh, ry, rx, k) if s is None else (G, rh, ry, rx, k, s)

    def follow(plan):
        for what in plan:
            if what[0] == "chunk":
                score(*what[1:])
            elif what[0] == "ring":
                rh, of_b, distance, way = what[1:]
                ring = (b1 if of_b else a1)[rh]
                if distance == 2:
                    ring.far(way)
                elif distance == 0:
                    ring.relay(way)
                else:
                    ring.near(way)
            elif what[0] == "send":
                src = what[1] if what[2][2] is None else what[1][:2] + what[2][2:3] + what[1][3:]
                posted[what[2]] = mail.post(piece(src), piece(what[2]), devices[what[3]])
            elif what[1] in posted:
                posted[what[1]].wait_recv()

    first_half = [(0, ((k, f), (k, f + 1))) for f in (2, 0) for k in (0, 1)]
    own_place, beside = (1, ((0, 0), (1, 0))), (1, ((0, 1), (0, 3), (1, 1), (1, 3)))
    rings = [(first_half, 2 * b + way, (0, b, d, way)) for d in (2, 1) for b in (0, 1) for way in (0, 1)]
    rings += [(first_half + [own_place], 2 * b + way, (0, b, 0, way)) for b in (0, 1) for way in (0, 1)]
    plan = gather_plan(first_half + [own_place, beside], rings)
    opening = next(n for n, what in enumerate(plan) if what[0] == "wait" and (what[1][0] or what[1][3] or what[1][4]))
    for k in (0, 1):
        posted[1, k, None, 0, 0] = mail.post((G, 0, 0, 0, k), (G, 1, 0, 0, k), mirror)
    follow(plan[:opening])
    whole = slice(None)
    for copy in fetched:
        copy.wait()
    shared = [
        mail.post((src, whole), (dst, whole), sibling)
        for src, dst in ((short_ref, short_in), (live_ref, live_in), (pos_ref, pos_in), (neg_ref, neg_in))
    ]
    shared.append(mail.post((emb2, pl.ds(0, docs)), (emb2, pl.ds(docs, docs)), sibling))
    embh[pl.ds(0, docs), :] = emb2[pl.ds(0, docs), :] * jnp.bfloat16(0.5)
    slot_weights(live_ref, pos_ref, neg_ref, sw, 0, panel, slots, nneg)
    eg[...] = jnp.zeros_like(eg)
    scoring = next(n for n, what in enumerate(plan) if what[0] == "chunk")
    follow(plan[opening:scoring])
    for copy in shared:
        copy.wait_recv()
    slot_weights(live_in, pos_in, neg_in, sw, 1, panel, slots, nneg)
    embh[pl.ds(docs, docs), :] = emb2[pl.ds(docs, docs), :] * jnp.bfloat16(0.5)
    follow(plan[scoring:])
    score(1, ((0, 2), (1, 2)))
    first_far(1)
    first_near(1)
    returned = mail.post((eg, pl.ds(docs, docs)), (eg_in, whole), sibling)
    first_relays(1)
    second_sends(0)
    second_sends(1)
    second_relays(0)
    returned.wait_recv()
    eg_ref[...] = eg[pl.ds(0, docs), :] + eg_in[...]
    second_relays(1)
    plane_sum(0)
    z_sends(0)
    plane_sum(1)
    z_sends(1)

    total = V[0, at.e]
    for k, copy in enumerate(slices):
        copy.wait_recv()
        total += z_in[k].astype(jnp.float32)
    part[at.e] = total * scale
    shares = [mail.post((part, at.e), (part, at.e), at.along_enc(k)) for k in range(1, 4)]
    for copy in shares:
        copy.wait_recv()
    wg_ref[...] = part[...].reshape(panel, width) * valid

    mail.finish()


def shards(embeddings, classifier, label_valid, shortlist, slot_live, positive, negative):
    lab_count = lax.axis_size("lab")
    enc_count = lax.axis_size("enc")
    docs, width = embeddings.shape
    panel = classifier.shape[0]
    slots = shortlist.shape[1]
    nneg = negative.shape[2]
    scale = 1.0 / math.sqrt(docs * enc_count * slots)
    by_slot = lambda a: a.transpose(1, 0)
    vmem, hbm = pl.BlockSpec(memory_space=pltpu.VMEM), pl.BlockSpec(memory_space=pl.ANY)
    bf16, f32 = jnp.bfloat16, jnp.float32
    piece = (16, width)
    return pl.pallas_call(
        functools.partial(kernel, scale, panel, slots, nneg),
        out_shape=(pltpu.VMEM((panel, width), f32), pltpu.VMEM((docs, width), f32)),
        in_specs=[hbm, vmem, vmem] + [hbm] * 4,
        out_specs=(vmem, vmem),
        scratch_shapes=[
            pltpu.VMEM((2, 4, 4, 2, 2) + piece, bf16),
            pltpu.VMEM((2 * docs, width), bf16),
            pltpu.VMEM((2 * docs, width), bf16),
            pltpu.VMEM((2, slots, panel, docs), f32),
            pltpu.VMEM((8 * panel, 2 * docs), bf16),
            pltpu.VMEM((2, 4, 4, 2, 2) + piece, f32),
            pltpu.VMEM((2 * docs, width), f32),
            pltpu.VMEM((docs, width), f32),
            pltpu.VMEM((slots, docs), jnp.int32),
            pltpu.VMEM((slots, docs), jnp.int32),
            pltpu.VMEM((slots, docs), jnp.int32),
            pltpu.VMEM((slots * nneg, docs), jnp.int32),
            pltpu.VMEM((slots, docs), jnp.int32),
            pltpu.VMEM((slots, docs), jnp.int32),
            pltpu.VMEM((slots, docs), jnp.int32),
            pltpu.VMEM((slots * nneg, docs), jnp.int32),
            pltpu.VMEM((2, 2, 3, 4) + piece, bf16),
            pltpu.VMEM((2, 2, 3, 4) + piece, bf16),
            pltpu.VMEM((2, 2, 3, 4) + piece, bf16),
            pltpu.VMEM((2, 2, 3, 4) + piece, bf16),
            pltpu.VMEM((2, 4, 2) + piece, f32),
            pltpu.VMEM((2, 4, 2) + piece, f32),
            pltpu.VMEM((2, 2, 3, 1) + piece, bf16),
            pltpu.VMEM((2, 2, 3, 1) + piece, bf16),
            pltpu.VMEM((2, 2, 3, 1) + piece, bf16),
            pltpu.VMEM((2, 2, 3, 1) + piece, bf16),
            pltpu.VMEM((2, 4) + piece, f32),
            pltpu.VMEM((2, 4) + piece, bf16),
            pltpu.VMEM((7,) + piece, bf16),
            pltpu.VMEM((4,) + piece, f32),
            pltpu.SemaphoreType.DMA((192,)),
            pltpu.SemaphoreType.DMA((192,)),
            pltpu.SemaphoreType.DMA((5,)),
        ],
        compiler_params=pltpu.CompilerParams(
            collective_id=0, has_side_effects=True, vmem_limit_bytes=60 * 1024 * 1024
        ),
        name="step",
    )(
        embeddings,
        classifier,
        label_valid.reshape(1, panel),
        by_slot(shortlist),
        by_slot(slot_live),
        by_slot(positive),
        negative.transpose(1, 2, 0).reshape(slots * nneg, docs),
    )


def solution(mesh):
    in_specs = (
        P(("enc", "lab"), None),
        P("lab", None),
        P("lab"),
        P(("enc", "lab"), None),
        P(("enc", "lab"), None),
        P(("enc", "lab"), None),
        P(("enc", "lab"), None, None),
    )
    out_specs = (P("lab", None), P(("enc", "lab"), None))
    return jax.shard_map(shards, mesh=mesh, in_specs=in_specs, out_specs=out_specs, check_vma=False)
```

```python
import functools
import heapq
import math

import jax
import jax.numpy as jnp
from jax import lax
from jax.experimental import pallas as pl
from jax.experimental.pallas import tpu as pltpu
from jax.sharding import PartitionSpec as P

MESH = pl.DeviceIdType.MESH
NT = (((1,), (1,)), ((), ()))
TN = (((0,), (0,)), ((), ()))


def rem4(v):
    return lax.rem(v + 8, 4)


class Place:
    def __init__(self):
        self.e = lax.axis_index("enc")
        lab = lax.axis_index("lab")
        self.c = lax.rem(lab, 2)
        self.x = lax.rem(lax.div(lab, 2), 4)
        self.y = lax.rem(lax.div(lab, 8), 4)
        self.h = lax.div(lab, 32)

    def lab_of(self, h, y, x, c):
        return ((h * 4 + y) * 4 + x) * 2 + c

    def along_x(self, k):
        return (self.e, self.lab_of(self.h, self.y, rem4(self.x + k), self.c))

    def along_y(self, k):
        return (self.e, self.lab_of(self.h, rem4(self.y + k), self.x, self.c))

    def sibling(self):
        return (self.e, self.lab_of(self.h, self.y, self.x, 1 - self.c))

    def mirror(self):
        return (3 - self.e, self.lab_of(1 - self.h, self.y, self.x, self.c))

    def across(self, k):
        return (rem4(self.e + k), self.lab_of(1 - self.h, self.y, self.x, self.c))

    def along_enc(self, k):
        return (rem4(self.e + k), self.lab_of(self.h, self.y, self.x, self.c))


class Copy:
    def __init__(self, mail, n, src, dst, device):
        self.mail, self.n, self.src, self.dst, self.device = mail, n, src, dst, device

    def made(self):
        return pltpu.make_async_remote_copy(
            src_ref=self.src[0].at[self.src[1:]],
            dst_ref=self.dst[0].at[self.dst[1:]],
            send_sem=self.mail.send.at[self.n],
            recv_sem=self.mail.recv.at[self.n],
            device_id=self.device,
            device_id_type=MESH,
        )

    def wait_recv(self):
        self.made().wait_recv()


class Mail:
    def __init__(self, send, recv):
        self.send, self.recv, self.sent = send, recv, []

    def post(self, src, dst, device):
        copy = Copy(self, len(self.sent), src, dst, device)
        copy.made().start()
        self.sent.append(copy)
        return copy

    def finish(self):
        for copy in self.sent:
            copy.made().wait_send()


RIGHT, LEFT, UP, DOWN = range(4)


def onward(key):
    rh, k, s, ry, rx = key
    first, second = (rx, ry) if k == 0 else (ry, rx)
    ways = ((RIGHT, LEFT), (UP, DOWN)) if k == 0 else ((UP, DOWN), (RIGHT, LEFT))

    def there(s, f, t):
        return (rh, k, s, t, f) if k == 0 else (rh, k, s, f, t)

    out = []
    if second == 0:
        if first == 0:
            out += [(ways[0][0], there(None, 3, 0), 4), (ways[0][1], there(None, 1, 0), 4)]
        elif first != 2:
            s = 0 if first == 3 else 1
            out += [(ways[0][s], there(s, 2, 0), 3)]
        out += [(ways[1][0], there(None, first, 3), 2), (ways[1][1], there(None, first, 1), 2)]
    elif second != 2:
        s = 0 if second == 3 else 1
        out += [(ways[1][s], there(s, first, 2), 1)]
    return out


def gather_plan(chunks, rings, wire=0.6, hop=3.2, chunk_time=0.95):
    plan, free, now = [], [0.0] * 4, 0.0
    events = [(0.0, k, (0, k, None, 0, 0)) for k in (0, 1)] + [(5.0 + 2.0 * k, 2 + k, (1, k, None, 0, 0)) for k in (0, 1)]
    heapq.heapify(events)
    order, have, todo, rings, first_ring = 4, set(), list(chunks), list(rings), 1e9

    def runnable():
        for rh, parts in todo:
            places = [(k, t, f) if k == 0 else (k, f, t) for k, f in parts for t in range(4)]
            if all((rh,) + place in have for place in places):
                return rh, parts
        return None

    while events or todo:
        chunk = runnable()
        quiet = not events or events[0][0] > now + 0.5 or min(free) > now + 1.5
        if chunk and quiet:
            todo.remove(chunk)
            plan.append(("chunk",) + chunk)
            now += chunk_time * len(chunk[1])
            continue
        for ring in list(rings):
            needs, way, message = ring
            if not any(rest in needs for rest in todo) and free[way] < now + 0.3:
                if message[2] == 0 and now < first_ring + 5.5:
                    continue
                first_ring = min(first_ring, now)
                rings.remove(ring)
                plan.append(("ring",) + message)
                free[way] = max(now, free[way]) + 8 * wire / 2
                now += 0.1
        if not events:
            now += 0.5
            continue
        now = max(now, events[0][0])
        sends = []
        while events and events[0][0] <= now:
            key = heapq.heappop(events)[2]
            plan.append(("wait", key))
            now += 0.03
            rh, k, s, ry, rx = key
            if s is not None:
                if (rh, k, 1 - s, ry, rx) not in have:
                    have.add(key)
                    continue
                key = (rh, k, None, ry, rx)
            have.add((rh, k, ry, rx))
            sends += [(-left, rh, way, key, then) for way, then, left in onward(key)]
        for _, _, way, key, then in sorted(sends, key=lambda send: send[:3]):
            free[way] = max(now, free[way]) + (wire if then[2] is not None else 2 * wire)
            heapq.heappush(events, (free[way] + hop, order, then))
            order += 1
            now += 0.03
            plan.append(("send", key, then, way))
    return plan + [("ring",) + message for _, _, message in rings]


class RingSum:
    def __init__(self, mail, out, into, rh, groups, value, plus, minus):
        self.mail, self.out, self.into, self.rh, self.groups, self.value = mail, out, into, rh, groups, value
        self.plus, self.minus = plus, minus
        self.copies = {}

    def fill(self, way, slot, make):
        def one(g, carry):
            self.out[self.rh, way, slot, g] = make(g).astype(jnp.bfloat16)
            return carry

        lax.fori_loop(0, self.groups, one, 0, unroll=True)
        self.copies[way, slot] = self.mail.post(
            (self.out, self.rh, way, slot), (self.into, self.rh, way, slot), self.minus if way else self.plus
        )

    def far(self, way):
        self.fill(way, 0, lambda g: self.value(g, 2, way))

    def near(self, way):
        self.fill(way, 1, lambda g: self.value(g, 3 if way else 1, 0 if way else 1))

    def got(self, way, slot, g):
        return self.into[self.rh, way, slot, g].astype(jnp.float32)

    def relay(self, way):
        self.copies[way, 0].wait_recv()
        self.fill(way, 2, lambda g: self.value(g, 3 if way else 1, way) + self.got(way, 0, g))

    def collect(self, store):
        for way in (0, 1):
            for slot in (1, 2):
                self.copies[way, slot].wait_recv()

        def one(g, carry):
            store(g, 0, self.value(g, 0, 0) + self.got(0, 2, g) + self.got(1, 1, g))
            store(g, 1, self.value(g, 0, 1) + self.got(0, 1, g) + self.got(1, 2, g))
            return carry

        lax.fori_loop(0, self.groups, one, 0, unroll=True)


def slot_weights(live_ref, pos_ref, neg_ref, sw, side, panel, slots, nneg):
    docs = pos_ref.shape[1]
    label = lax.broadcasted_iota(jnp.int32, (panel, docs), 0)
    for s in range(slots):
        hot = jnp.where(pos_ref[pl.ds(s, 1), :] == label, 1.0, 0.0)
        count = hot
        for k in range(nneg):
            count += jnp.where(neg_ref[pl.ds(s * nneg + k, 1), :] == label, 1.0, 0.0)
        half = 0.5 * live_ref[pl.ds(s, 1), :].astype(jnp.float32)
        sw[side, s] = half * count * (1.0 - 2.0 * hot)


def kernel(
    scale, panel, slots, nneg,
    emb_hbm, cls_ref, valid_ref, short_hbm, live_hbm, pos_hbm, neg_hbm,
    wg_ref, eg_ref,
    G, emb2, embh, sw, dl, K, eg, eg_in, short_ref, live_ref, pos_ref, neg_ref, short_in, live_in, pos_in, neg_in,
    a1_out, a1_in, b1_out, b1_in, sum_a, sum_b, a2_out, a2_in, b2_out, b2_in,
    V, z_out, z_in, part,
    send, recv, fetch,
):
    at = Place()
    docs, width = emb_hbm.shape
    right, left, up, down = at.along_x(1), at.along_x(-1), at.along_y(1), at.along_y(-1)
    sibling = at.sibling()
    barrier = pltpu.get_barrier_semaphore()
    partners = [right, left, up, down, sibling]
    partners += [at.along_enc(k) for k in range(1, 4)] + [at.across(k) for k in range(4)]
    for device in partners:
        pl.semaphore_signal(barrier, inc=1, device_id=device, device_id_type=MESH)

    emb_ref = emb2.at[pl.ds(0, docs)]
    fetched = [
        pltpu.make_async_copy(src, dst, fetch.at[n])
        for n, (src, dst) in enumerate(
            (
                (short_hbm, short_ref),
                (live_hbm, live_ref),
                (pos_hbm, pos_ref),
                (neg_hbm, neg_ref),
                (emb_hbm, emb_ref),
            )
        )
    ]
    for copy in fetched:
        copy.start()

    rows = lax.broadcasted_iota(jnp.int32, (panel, panel), 0)
    cols = lax.broadcasted_iota(jnp.int32, (panel, panel), 1)
    flags = jnp.where(rows == cols, valid_ref[...].astype(jnp.float32), 0.0)
    valid = jnp.sum(flags, axis=1, keepdims=True)
    mine = (cls_ref[...] * valid).astype(jnp.bfloat16)
    G[0, 0, 0] = mine.reshape(2, 2, 16, width)
    pl.semaphore_wait(barrier, len(partners))

    mail = Mail(send, recv)

    def score(rh, parts):
        w = [G[rh, :, f, 0] if k == 0 else G[rh, f, :, 1] for k, f in parts]
        w = jnp.concatenate([block.reshape(2 * panel, width) for block in w], axis=0)
        labels = w.shape[0]
        half_logits = lax.dot_general(w, embh[...], NT, preferred_element_type=jnp.float32)
        h = at.h if rh == 0 else 1 - at.h
        row = 0
        for k, f in parts:
            for t in range(4):
                ry, rx = (t, f) if k == 0 else (f, t)
                cluster = at.lab_of(h, rem4(at.y + ry), rem4(at.x + rx), at.c)
                for side, short in enumerate((short_ref, short_in)):
                    hw = None
                    for s in range(slots):
                        term = sw[side, s, pl.ds(k * panel // 2, panel // 2)] * jnp.where(
                            short[pl.ds(s, 1), :] == cluster, 1.0, 0.0
                        )
                        hw = term if hw is None else hw + term
                    t = jnp.tanh(half_logits[row : row + panel // 2, side * docs : (side + 1) * docs])
                    dl[pl.ds(row, panel // 2), pl.ds(side * docs, docs)] = (jnp.abs(hw) * t + hw).astype(jnp.bfloat16)
                row += panel // 2
        d = dl[pl.ds(0, labels), :]
        grad = jnp.dot(d, emb2[...], preferred_element_type=jnp.float32)
        for n, (k, f) in enumerate(parts):
            part_grad = grad[n * 2 * panel : (n + 1) * 2 * panel].reshape(4, 2, 16, width)
            if k == 0:
                K[rh, :, f, 0] = part_grad
            else:
                K[rh, f, :, 1] = part_grad
        eg[...] += lax.dot_general(d, w, TN, preferred_element_type=jnp.float32)

    def term_a(rh):
        return lambda g, rel, s: K[rh, g, rel, 0, s]

    def term_b(rh):
        return lambda g, rel, s: K[rh, rel, g, 1, s]

    def ring(out, into, rh, groups, value, plus, minus):
        return RingSum(mail, out, into, rh, groups, value, plus, minus)

    a1 = [ring(a1_out, a1_in, rh, 4, term_a(rh), right, left) for rh in (0, 1)]
    b1 = [ring(b1_out, b1_in, rh, 4, term_b(rh), up, down) for rh in (0, 1)]
    a2 = [ring(a2_out, a2_in, rh, 1, lambda g, rel, s, rh=rh: sum_a[rh, rel, s], up, down) for rh in (0, 1)]
    b2 = [ring(b2_out, b2_in, rh, 1, lambda g, rel, s, rh=rh: sum_b[rh, rel, s], right, left) for rh in (0, 1)]

    def first_far(rh):
        for way in (0, 1):
            a1[rh].far(way)
            b1[rh].far(way)

    def first_near(rh):
        for way in (0, 1):
            a1[rh].near(way)
            b1[rh].near(way)

    def first_relays(rh):
        for way in (0, 1):
            a1[rh].relay(way)
            b1[rh].relay(way)

    def second_sends(rh):
        def store_a(g, s, v):
            sum_a[rh, g, s] = v

        def store_b(g, s, v):
            sum_b[rh, g, s] = v

        a1[rh].collect(store_a)
        for way in (0, 1):
            a2[rh].far(way)
        b1[rh].collect(store_b)
        for way in (0, 1):
            b2[rh].far(way)
        for way in (0, 1):
            a2[rh].near(way)
            b2[rh].near(way)

    def second_relays(rh):
        for way in (0, 1):
            a2[rh].relay(way)
            b2[rh].relay(way)

    def plane_sum(rh):
        def store(half):
            def put(g, s, v):
                V[rh, 2 * half + s] = v
                z_out[rh, 2 * half + s] = v.astype(jnp.bfloat16)

            return put

        a2[rh].collect(store(0))
        b2[rh].collect(store(1))

    slices = []

    def z_sends(rh):
        for k in range(1 - rh, 4):
            device = at.across(k) if rh else at.along_enc(k)
            slices.append(mail.post((z_out, rh, rem4(at.e + k)), (z_in, len(slices)), device))

    posted = {}
    devices = (right, left, up, down)
    mirror = at.mirror()

    def piece(key):
        rh, k, s, ry, rx = key
        return (G, rh, ry, rx, k) if s is None else (G, rh, ry, rx, k, s)

    def follow(plan):
        for what in plan:
            if what[0] == "chunk":
                score(*what[1:])
            elif what[0] == "ring":
                rh, of_b, distance, way = what[1:]
                ring = (b1 if of_b else a1)[rh]
                if distance == 2:
                    ring.far(way)
                elif distance == 0:
                    ring.relay(way)
                else:
                    ring.near(way)
            elif what[0] == "send":
                src = what[1] if what[2][2] is None else what[1][:2] + what[2][2:3] + what[1][3:]
                posted[what[2]] = mail.post(piece(src), piece(what[2]), devices[what[3]])
            elif what[1] in posted:
                posted[what[1]].wait_recv()

    first_half = [(0, ((0, f), (0, f + 1), (1, f), (1, f + 1))) for f in (0, 2)]
    own_place, beside = (1, ((0, 0), (1, 0))), (1, ((0, 1), (0, 3), (1, 1), (1, 3)))
    rings = [(first_half, 2 * b + way, (0, b, d, way)) for d in (2, 1) for b in (0, 1) for way in (0, 1)]
    rings += [(first_half + [own_place], 2 * b + way, (0, b, 0, way)) for b in (0, 1) for way in (0, 1)]
    plan = gather_plan(first_half + [own_place, beside], rings)
    opening = next(n for n, what in enumerate(plan) if what[0] == "wait" and (what[1][0] or what[1][3] or what[1][4]))
    for k in (0, 1):
        posted[1, k, None, 0, 0] = mail.post((G, 0, 0, 0, k), (G, 1, 0, 0, k), mirror)
    follow(plan[:opening])
    whole = slice(None)
    for copy in fetched:
        copy.wait()
    shared = [
        mail.post((src, whole), (dst, whole), sibling)
        for src, dst in ((short_ref, short_in), (live_ref, live_in), (pos_ref, pos_in), (neg_ref, neg_in))
    ]
    shared.append(mail.post((emb2, pl.ds(0, docs)), (emb2, pl.ds(docs, docs)), sibling))
    embh[pl.ds(0, docs), :] = emb2[pl.ds(0, docs), :] * jnp.bfloat16(0.5)
    slot_weights(live_ref, pos_ref, neg_ref, sw, 0, panel, slots, nneg)
    eg[...] = jnp.zeros_like(eg)
    scoring = next(n for n, what in enumerate(plan) if what[0] == "chunk")
    follow(plan[opening:scoring])
    for copy in shared:
        copy.wait_recv()
    slot_weights(live_in, pos_in, neg_in, sw, 1, panel, slots, nneg)
    embh[pl.ds(docs, docs), :] = emb2[pl.ds(docs, docs), :] * jnp.bfloat16(0.5)
    follow(plan[scoring:])
    score(1, ((0, 2), (1, 2)))
    first_far(1)
    first_near(1)
    returned = mail.post((eg, pl.ds(docs, docs)), (eg_in, whole), sibling)
    first_relays(1)
    second_sends(0)
    second_sends(1)
    second_relays(0)
    returned.wait_recv()
    eg_ref[...] = eg[pl.ds(0, docs), :] + eg_in[...]
    second_relays(1)
    plane_sum(0)
    z_sends(0)
    plane_sum(1)
    z_sends(1)

    total = V[0, at.e]
    for k, copy in enumerate(slices):
        copy.wait_recv()
        total += z_in[k].astype(jnp.float32)
    part[at.e] = total * scale
    shares = [mail.post((part, at.e), (part, at.e), at.along_enc(k)) for k in range(1, 4)]
    for copy in shares:
        copy.wait_recv()
    wg_ref[...] = part[...].reshape(panel, width) * valid

    mail.finish()


def shards(embeddings, classifier, label_valid, shortlist, slot_live, positive, negative):
    lab_count = lax.axis_size("lab")
    enc_count = lax.axis_size("enc")
    docs, width = embeddings.shape
    panel = classifier.shape[0]
    slots = shortlist.shape[1]
    nneg = negative.shape[2]
    scale = 1.0 / math.sqrt(docs * enc_count * slots)
    by_slot = lambda a: a.transpose(1, 0)
    vmem, hbm = pl.BlockSpec(memory_space=pltpu.VMEM), pl.BlockSpec(memory_space=pl.ANY)
    bf16, f32 = jnp.bfloat16, jnp.float32
    piece = (16, width)
    return pl.pallas_call(
        functools.partial(kernel, scale, panel, slots, nneg),
        out_shape=(pltpu.VMEM((panel, width), f32), pltpu.VMEM((docs, width), f32)),
        in_specs=[hbm, vmem, vmem] + [hbm] * 4,
        out_specs=(vmem, vmem),
        scratch_shapes=[
            pltpu.VMEM((2, 4, 4, 2, 2) + piece, bf16),
            pltpu.VMEM((2 * docs, width), bf16),
            pltpu.VMEM((2 * docs, width), bf16),
            pltpu.VMEM((2, slots, panel, docs), f32),
            pltpu.VMEM((8 * panel, 2 * docs), bf16),
            pltpu.VMEM((2, 4, 4, 2, 2) + piece, f32),
            pltpu.VMEM((2 * docs, width), f32),
            pltpu.VMEM((docs, width), f32),
            pltpu.VMEM((slots, docs), jnp.int32),
            pltpu.VMEM((slots, docs), jnp.int32),
            pltpu.VMEM((slots, docs), jnp.int32),
            pltpu.VMEM((slots * nneg, docs), jnp.int32),
            pltpu.VMEM((slots, docs), jnp.int32),
            pltpu.VMEM((slots, docs), jnp.int32),
            pltpu.VMEM((slots, docs), jnp.int32),
            pltpu.VMEM((slots * nneg, docs), jnp.int32),
            pltpu.VMEM((2, 2, 3, 4) + piece, bf16),
            pltpu.VMEM((2, 2, 3, 4) + piece, bf16),
            pltpu.VMEM((2, 2, 3, 4) + piece, bf16),
            pltpu.VMEM((2, 2, 3, 4) + piece, bf16),
            pltpu.VMEM((2, 4, 2) + piece, f32),
            pltpu.VMEM((2, 4, 2) + piece, f32),
            pltpu.VMEM((2, 2, 3, 1) + piece, bf16),
            pltpu.VMEM((2, 2, 3, 1) + piece, bf16),
            pltpu.VMEM((2, 2, 3, 1) + piece, bf16),
            pltpu.VMEM((2, 2, 3, 1) + piece, bf16),
            pltpu.VMEM((2, 4) + piece, f32),
            pltpu.VMEM((2, 4) + piece, bf16),
            pltpu.VMEM((7,) + piece, bf16),
            pltpu.VMEM((4,) + piece, f32),
            pltpu.SemaphoreType.DMA((192,)),
            pltpu.SemaphoreType.DMA((192,)),
            pltpu.SemaphoreType.DMA((5,)),
        ],
        compiler_params=pltpu.CompilerParams(
            collective_id=0, has_side_effects=True, vmem_limit_bytes=60 * 1024 * 1024
        ),
        name="step",
    )(
        embeddings,
        classifier,
        label_valid.reshape(1, panel),
        by_slot(shortlist),
        by_slot(slot_live),
        by_slot(positive),
        negative.transpose(1, 2, 0).reshape(slots * nneg, docs),
    )


def solution(mesh):
    in_specs = (
        P(("enc", "lab"), None),
        P("lab", None),
        P("lab"),
        P(("enc", "lab"), None),
        P(("enc", "lab"), None),
        P(("enc", "lab"), None),
        P(("enc", "lab"), None, None),
    )
    out_specs = (P("lab", None), P(("enc", "lab"), None))
    return jax.shard_map(shards, mesh=mesh, in_specs=in_specs, out_specs=out_specs, check_vma=False)
```

```python
import functools
import heapq
import math

import jax
import jax.numpy as jnp
from jax import lax
from jax.experimental import pallas as pl
from jax.experimental.pallas import tpu as pltpu
from jax.sharding import PartitionSpec as P

MESH = pl.DeviceIdType.MESH
NT = (((1,), (1,)), ((), ()))
TN = (((0,), (0,)), ((), ()))


def rem4(v):
    return lax.rem(v + 8, 4)


class Place:
    def __init__(self):
        self.e = lax.axis_index("enc")
        lab = lax.axis_index("lab")
        self.c = lax.rem(lab, 2)
        self.x = lax.rem(lax.div(lab, 2), 4)
        self.y = lax.rem(lax.div(lab, 8), 4)
        self.h = lax.div(lab, 32)

    def lab_of(self, h, y, x, c):
        return ((h * 4 + y) * 4 + x) * 2 + c

    def along_x(self, k):
        return (self.e, self.lab_of(self.h, self.y, rem4(self.x + k), self.c))

    def along_y(self, k):
        return (self.e, self.lab_of(self.h, rem4(self.y + k), self.x, self.c))

    def sibling(self):
        return (self.e, self.lab_of(self.h, self.y, self.x, 1 - self.c))

    def mirror(self):
        return (3 - self.e, self.lab_of(1 - self.h, self.y, self.x, self.c))

    def across(self, k):
        return (rem4(self.e + k), self.lab_of(1 - self.h, self.y, self.x, self.c))

    def along_enc(self, k):
        return (rem4(self.e + k), self.lab_of(self.h, self.y, self.x, self.c))


class Copy:
    def __init__(self, mail, n, src, dst, device):
        self.mail, self.n, self.src, self.dst, self.device = mail, n, src, dst, device

    def made(self):
        return pltpu.make_async_remote_copy(
            src_ref=self.src[0].at[self.src[1:]],
            dst_ref=self.dst[0].at[self.dst[1:]],
            send_sem=self.mail.send.at[self.n],
            recv_sem=self.mail.recv.at[self.n],
            device_id=self.device,
            device_id_type=MESH,
        )

    def wait_recv(self):
        self.made().wait_recv()


class Mail:
    def __init__(self, send, recv):
        self.send, self.recv, self.sent = send, recv, []

    def post(self, src, dst, device):
        copy = Copy(self, len(self.sent), src, dst, device)
        copy.made().start()
        self.sent.append(copy)
        return copy

    def finish(self):
        for copy in self.sent:
            copy.made().wait_send()


RIGHT, LEFT, UP, DOWN = range(4)


def onward(key):
    rh, k, s, ry, rx = key
    first, second = (rx, ry) if k == 0 else (ry, rx)
    ways = ((RIGHT, LEFT), (UP, DOWN)) if k == 0 else ((UP, DOWN), (RIGHT, LEFT))

    def there(s, f, t):
        return (rh, k, s, t, f) if k == 0 else (rh, k, s, f, t)

    out = []
    if second == 0:
        if first == 0:
            out += [(ways[0][0], there(None, 3, 0), 4), (ways[0][1], there(None, 1, 0), 4)]
        elif first != 2:
            s = 0 if first == 3 else 1
            out += [(ways[0][s], there(s, 2, 0), 3)]
        out += [(ways[1][0], there(None, first, 3), 2), (ways[1][1], there(None, first, 1), 2)]
    elif second != 2:
        s = 0 if second == 3 else 1
        out += [(ways[1][s], there(s, first, 2), 1)]
    return out


def gather_plan(chunks, rings, wire=0.6, hop=3.2, chunk_time=0.95):
    plan, free, now = [], [0.0] * 4, 0.0
    events = [(0.0, k, (0, k, None, 0, 0)) for k in (0, 1)] + [(5.0 + 2.0 * k, 2 + k, (1, k, None, 0, 0)) for k in (0, 1)]
    heapq.heapify(events)
    order, have, todo, rings, first_ring = 4, set(), list(chunks), list(rings), 1e9

    def runnable():
        for rh, parts in todo:
            places = [(k, t, f) if k == 0 else (k, f, t) for k, f in parts for t in range(4)]
            if all((rh,) + place in have for place in places):
                return rh, parts
        return None

    while events or todo:
        chunk = runnable()
        quiet = not events or events[0][0] > now + 0.5 or min(free) > now + 1.5
        if chunk and quiet:
            todo.remove(chunk)
            plan.append(("chunk",) + chunk)
            now += chunk_time * len(chunk[1])
            continue
        for ring in list(rings):
            needs, way, message = ring
            if not any(rest in needs for rest in todo) and free[way] < now + 0.3:
                if message[2] == 0 and now < first_ring + 5.5:
                    continue
                first_ring = min(first_ring, now)
                rings.remove(ring)
                plan.append(("ring",) + message)
                free[way] = max(now, free[way]) + 8 * wire / 2
                now += 0.1
        if not events:
            now += 0.5
            continue
        now = max(now, events[0][0])
        sends = []
        while events and events[0][0] <= now:
            key = heapq.heappop(events)[2]
            plan.append(("wait", key))
            now += 0.03
            rh, k, s, ry, rx = key
            if s is not None:
                if (rh, k, 1 - s, ry, rx) not in have:
                    have.add(key)
                    continue
                key = (rh, k, None, ry, rx)
            have.add((rh, k, ry, rx))
            sends += [(-left, rh, way, key, then) for way, then, left in onward(key)]
        for _, _, way, key, then in sorted(sends, key=lambda send: send[:3]):
            free[way] = max(now, free[way]) + (wire if then[2] is not None else 2 * wire)
            heapq.heappush(events, (free[way] + hop, order, then))
            order += 1
            now += 0.03
            plan.append(("send", key, then, way))
    return plan + [("ring",) + message for _, _, message in rings]


class RingSum:
    def __init__(self, mail, out, into, rh, groups, value, plus, minus):
        self.mail, self.out, self.into, self.rh, self.groups, self.value = mail, out, into, rh, groups, value
        self.plus, self.minus = plus, minus
        self.copies = {}

    def fill(self, way, slot, make):
        def one(g, carry):
            self.out[self.rh, way, slot, g] = make(g).astype(jnp.bfloat16)
            return carry

        lax.fori_loop(0, self.groups, one, 0, unroll=True)
        self.copies[way, slot] = self.mail.post(
            (self.out, self.rh, way, slot), (self.into, self.rh, way, slot), self.minus if way else self.plus
        )

    def far(self, way):
        self.fill(way, 0, lambda g: self.value(g, 2, way))

    def near(self, way):
        self.fill(way, 1, lambda g: self.value(g, 3 if way else 1, 0 if way else 1))

    def got(self, way, slot, g):
        return self.into[self.rh, way, slot, g].astype(jnp.float32)

    def relay(self, way):
        self.copies[way, 0].wait_recv()
        self.fill(way, 2, lambda g: self.value(g, 3 if way else 1, way) + self.got(way, 0, g))

    def collect(self, store):
        for way in (0, 1):
            for slot in (1, 2):
                self.copies[way, slot].wait_recv()

        def one(g, carry):
            store(g, 0, self.value(g, 0, 0) + self.got(0, 2, g) + self.got(1, 1, g))
            store(g, 1, self.value(g, 0, 1) + self.got(0, 1, g) + self.got(1, 2, g))
            return carry

        lax.fori_loop(0, self.groups, one, 0, unroll=True)


def slot_weights(live_ref, pos_ref, neg_ref, sw, side, panel, slots, nneg):
    docs = pos_ref.shape[1]
    label = lax.broadcasted_iota(jnp.int32, (panel, docs), 0)
    for s in range(slots):
        hot = jnp.where(pos_ref[pl.ds(s, 1), :] == label, 1.0, 0.0)
        count = hot
        for k in range(nneg):
            count += jnp.where(neg_ref[pl.ds(s * nneg + k, 1), :] == label, 1.0, 0.0)
        half = 0.5 * live_ref[pl.ds(s, 1), :].astype(jnp.float32)
        sw[side, s] = half * count * (1.0 - 2.0 * hot)


def kernel(
    scale, panel, slots, nneg,
    emb_hbm, cls_ref, valid_ref, short_hbm, live_hbm, pos_hbm, neg_hbm,
    wg_ref, eg_ref,
    G, emb2, embh, sw, dl, K, eg, eg_in, short_ref, live_ref, pos_ref, neg_ref, short_in, live_in, pos_in, neg_in,
    a1_out, a1_in, b1_out, b1_in, sum_a, sum_b, a2_out, a2_in, b2_out, b2_in,
    V, z_out, z_in, part,
    send, recv, fetch,
):
    at = Place()
    docs, width = emb_hbm.shape
    right, left, up, down = at.along_x(1), at.along_x(-1), at.along_y(1), at.along_y(-1)
    sibling = at.sibling()
    barrier = pltpu.get_barrier_semaphore()
    partners = [right, left, up, down, sibling]
    partners += [at.along_enc(k) for k in range(1, 4)] + [at.across(k) for k in range(4)]
    for device in partners:
        pl.semaphore_signal(barrier, inc=1, device_id=device, device_id_type=MESH)

    emb_ref = emb2.at[pl.ds(0, docs)]
    fetched = [
        pltpu.make_async_copy(src, dst, fetch.at[n])
        for n, (src, dst) in enumerate(
            (
                (short_hbm, short_ref),
                (live_hbm, live_ref),
                (pos_hbm, pos_ref),
                (neg_hbm, neg_ref),
                (emb_hbm, emb_ref),
            )
        )
    ]
    for copy in fetched:
        copy.start()

    rows = lax.broadcasted_iota(jnp.int32, (panel, panel), 0)
    cols = lax.broadcasted_iota(jnp.int32, (panel, panel), 1)
    flags = jnp.where(rows == cols, valid_ref[...].astype(jnp.float32), 0.0)
    valid = jnp.sum(flags, axis=1, keepdims=True)
    mine = (cls_ref[...] * valid).astype(jnp.bfloat16)
    G[0, 0, 0] = mine.reshape(2, 2, 16, width)
    pl.semaphore_wait(barrier, len(partners))

    mail = Mail(send, recv)

    def score(rh, parts):
        w = [G[rh, :, f, 0] if k == 0 else G[rh, f, :, 1] for k, f in parts]
        w = jnp.concatenate([block.reshape(2 * panel, width) for block in w], axis=0)
        labels = w.shape[0]
        half_logits = lax.dot_general(w, embh[...], NT, preferred_element_type=jnp.float32)
        h = at.h if rh == 0 else 1 - at.h
        row = 0
        for k, f in parts:
            for t in range(4):
                ry, rx = (t, f) if k == 0 else (f, t)
                cluster = at.lab_of(h, rem4(at.y + ry), rem4(at.x + rx), at.c)
                for side, short in enumerate((short_ref, short_in)):
                    hw = None
                    for s in range(slots):
                        term = sw[side, s, pl.ds(k * panel // 2, panel // 2)] * jnp.where(
                            short[pl.ds(s, 1), :] == cluster, 1.0, 0.0
                        )
                        hw = term if hw is None else hw + term
                    t = jnp.tanh(half_logits[row : row + panel // 2, side * docs : (side + 1) * docs])
                    dl[pl.ds(row, panel // 2), pl.ds(side * docs, docs)] = (jnp.abs(hw) * t + hw).astype(jnp.bfloat16)
                row += panel // 2
        d = dl[pl.ds(0, labels), :]
        grad = jnp.dot(d, emb2[...], preferred_element_type=jnp.float32)
        for n, (k, f) in enumerate(parts):
            part_grad = grad[n * 2 * panel : (n + 1) * 2 * panel].reshape(4, 2, 16, width)
            if k == 0:
                K[rh, :, f, 0] = part_grad
            else:
                K[rh, f, :, 1] = part_grad
        eg[...] += lax.dot_general(d, w, TN, preferred_element_type=jnp.float32)

    def term_a(rh):
        return lambda g, rel, s: K[rh, g, rel, 0, s]

    def term_b(rh):
        return lambda g, rel, s: K[rh, rel, g, 1, s]

    def ring(out, into, rh, groups, value, plus, minus):
        return RingSum(mail, out, into, rh, groups, value, plus, minus)

    a1 = [ring(a1_out, a1_in, rh, 4, term_a(rh), right, left) for rh in (0, 1)]
    b1 = [ring(b1_out, b1_in, rh, 4, term_b(rh), up, down) for rh in (0, 1)]
    a2 = [ring(a2_out, a2_in, rh, 1, lambda g, rel, s, rh=rh: sum_a[rh, rel, s], up, down) for rh in (0, 1)]
    b2 = [ring(b2_out, b2_in, rh, 1, lambda g, rel, s, rh=rh: sum_b[rh, rel, s], right, left) for rh in (0, 1)]

    def first_far(rh):
        for way in (0, 1):
            a1[rh].far(way)
            b1[rh].far(way)

    def first_near(rh):
        for way in (0, 1):
            a1[rh].near(way)
            b1[rh].near(way)

    def first_relays(rh):
        for way in (0, 1):
            a1[rh].relay(way)
            b1[rh].relay(way)

    def second_sends(rh):
        def store_a(g, s, v):
            sum_a[rh, g, s] = v

        def store_b(g, s, v):
            sum_b[rh, g, s] = v

        a1[rh].collect(store_a)
        for way in (0, 1):
            a2[rh].far(way)
        b1[rh].collect(store_b)
        for way in (0, 1):
            b2[rh].far(way)
        for way in (0, 1):
            a2[rh].near(way)
            b2[rh].near(way)

    def second_relays(rh):
        for way in (0, 1):
            a2[rh].relay(way)
            b2[rh].relay(way)

    def plane_sum(rh):
        def store(half):
            def put(g, s, v):
                V[rh, 2 * half + s] = v
                z_out[rh, 2 * half + s] = v.astype(jnp.bfloat16)

            return put

        a2[rh].collect(store(0))
        b2[rh].collect(store(1))

    slices = []

    def z_sends(rh):
        for k in range(1 - rh, 4):
            device = at.across(k) if rh else at.along_enc(k)
            slices.append(mail.post((z_out, rh, rem4(at.e + k)), (z_in, len(slices)), device))

    posted = {}
    devices = (right, left, up, down)
    mirror = at.mirror()

    def piece(key):
        rh, k, s, ry, rx = key
        return (G, rh, ry, rx, k) if s is None else (G, rh, ry, rx, k, s)

    def follow(plan):
        for what in plan:
            if what[0] == "chunk":
                score(*what[1:])
            elif what[0] == "ring":
                rh, of_b, distance, way = what[1:]
                ring = (b1 if of_b else a1)[rh]
                if distance == 2:
                    ring.far(way)
                elif distance == 0:
                    ring.relay(way)
                else:
                    ring.near(way)
            elif what[0] == "send":
                src = what[1] if what[2][2] is None else what[1][:2] + what[2][2:3] + what[1][3:]
                posted[what[2]] = mail.post(piece(src), piece(what[2]), devices[what[3]])
            elif what[1] in posted:
                posted[what[1]].wait_recv()

    first_half = [(0, ((0, f), (0, f + 1), (1, f), (1, f + 1))) for f in (0, 2)]
    own_place, beside = (1, ((0, 0), (1, 0))), (1, ((0, 1), (0, 3), (1, 1), (1, 3)))
    rings = [(first_half, 2 * b + way, (0, b, d, way)) for d in (2, 1) for b in (0, 1) for way in (0, 1)]
    rings += [(first_half + [own_place], 2 * b + way, (0, b, 0, way)) for b in (0, 1) for way in (0, 1)]
    plan = gather_plan(first_half + [own_place, beside], rings)
    opening = next(n for n, what in enumerate(plan) if what[0] == "wait" and (what[1][0] or what[1][3] or what[1][4]))
    for k in (0, 1):
        posted[1, k, None, 0, 0] = mail.post((G, 0, 0, 0, k), (G, 1, 0, 0, k), mirror)
    follow(plan[:opening])
    whole = slice(None)
    for copy in fetched:
        copy.wait()
    shared = [
        mail.post((src, whole), (dst, whole), sibling)
        for src, dst in ((short_ref, short_in), (live_ref, live_in), (pos_ref, pos_in), (neg_ref, neg_in))
    ]
    shared.append(mail.post((emb2, pl.ds(0, docs)), (emb2, pl.ds(docs, docs)), sibling))
    embh[pl.ds(0, docs), :] = emb2[pl.ds(0, docs), :] * jnp.bfloat16(0.5)
    slot_weights(live_ref, pos_ref, neg_ref, sw, 0, panel, slots, nneg)
    eg[...] = jnp.zeros_like(eg)
    scoring = next(n for n, what in enumerate(plan) if what[0] == "chunk")
    follow(plan[opening:scoring])
    for copy in shared:
        copy.wait_recv()
    slot_weights(live_in, pos_in, neg_in, sw, 1, panel, slots, nneg)
    embh[pl.ds(docs, docs), :] = emb2[pl.ds(docs, docs), :] * jnp.bfloat16(0.5)
    follow(plan[scoring:])
    score(1, ((0, 2), (1, 2)))
    first_far(1)
    first_near(1)
    returned = mail.post((eg, pl.ds(docs, docs)), (eg_in, whole), sibling)
    first_relays(1)
    second_sends(0)
    second_sends(1)
    second_relays(0)
    second_relays(1)
    plane_sum(0)
    z_sends(0)
    plane_sum(1)
    z_sends(1)

    returned.wait_recv()
    eg_ref[...] = eg[pl.ds(0, docs), :] + eg_in[...]
    total = V[0, at.e]
    for k, copy in enumerate(slices):
        copy.wait_recv()
        total += z_in[k].astype(jnp.float32)
    part[at.e] = total * scale
    shares = [mail.post((part, at.e), (part, at.e), at.along_enc(k)) for k in range(1, 4)]
    for copy in shares:
        copy.wait_recv()
    wg_ref[...] = part[...].reshape(panel, width) * valid

    mail.finish()


def shards(embeddings, classifier, label_valid, shortlist, slot_live, positive, negative):
    lab_count = lax.axis_size("lab")
    enc_count = lax.axis_size("enc")
    docs, width = embeddings.shape
    panel = classifier.shape[0]
    slots = shortlist.shape[1]
    nneg = negative.shape[2]
    scale = 1.0 / math.sqrt(docs * enc_count * slots)
    by_slot = lambda a: a.transpose(1, 0)
    vmem, hbm = pl.BlockSpec(memory_space=pltpu.VMEM), pl.BlockSpec(memory_space=pl.ANY)
    bf16, f32 = jnp.bfloat16, jnp.float32
    piece = (16, width)
    return pl.pallas_call(
        functools.partial(kernel, scale, panel, slots, nneg),
        out_shape=(pltpu.VMEM((panel, width), f32), pltpu.VMEM((docs, width), f32)),
        in_specs=[hbm, vmem, vmem] + [hbm] * 4,
        out_specs=(vmem, vmem),
        scratch_shapes=[
            pltpu.VMEM((2, 4, 4, 2, 2) + piece, bf16),
            pltpu.VMEM((2 * docs, width), bf16),
            pltpu.VMEM((2 * docs, width), bf16),
            pltpu.VMEM((2, slots, panel, docs), f32),
            pltpu.VMEM((8 * panel, 2 * docs), bf16),
            pltpu.VMEM((2, 4, 4, 2, 2) + piece, f32),
            pltpu.VMEM((2 * docs, width), f32),
            pltpu.VMEM((docs, width), f32),
            pltpu.VMEM((slots, docs), jnp.int32),
            pltpu.VMEM((slots, docs), jnp.int32),
            pltpu.VMEM((slots, docs), jnp.int32),
            pltpu.VMEM((slots * nneg, docs), jnp.int32),
            pltpu.VMEM((slots, docs), jnp.int32),
            pltpu.VMEM((slots, docs), jnp.int32),
            pltpu.VMEM((slots, docs), jnp.int32),
            pltpu.VMEM((slots * nneg, docs), jnp.int32),
            pltpu.VMEM((2, 2, 3, 4) + piece, bf16),
            pltpu.VMEM((2, 2, 3, 4) + piece, bf16),
            pltpu.VMEM((2, 2, 3, 4) + piece, bf16),
            pltpu.VMEM((2, 2, 3, 4) + piece, bf16),
            pltpu.VMEM((2, 4, 2) + piece, f32),
            pltpu.VMEM((2, 4, 2) + piece, f32),
            pltpu.VMEM((2, 2, 3, 1) + piece, bf16),
            pltpu.VMEM((2, 2, 3, 1) + piece, bf16),
            pltpu.VMEM((2, 2, 3, 1) + piece, bf16),
            pltpu.VMEM((2, 2, 3, 1) + piece, bf16),
            pltpu.VMEM((2, 4) + piece, f32),
            pltpu.VMEM((2, 4) + piece, bf16),
            pltpu.VMEM((7,) + piece, bf16),
            pltpu.VMEM((4,) + piece, f32),
            pltpu.SemaphoreType.DMA((192,)),
            pltpu.SemaphoreType.DMA((192,)),
            pltpu.SemaphoreType.DMA((5,)),
        ],
        compiler_params=pltpu.CompilerParams(
            collective_id=0, has_side_effects=True, vmem_limit_bytes=60 * 1024 * 1024
        ),
        name="step",
    )(
        embeddings,
        classifier,
        label_valid.reshape(1, panel),
        by_slot(shortlist),
        by_slot(slot_live),
        by_slot(positive),
        negative.transpose(1, 2, 0).reshape(slots * nneg, docs),
    )


def solution(mesh):
    in_specs = (
        P(("enc", "lab"), None),
        P("lab", None),
        P("lab"),
        P(("enc", "lab"), None),
        P(("enc", "lab"), None),
        P(("enc", "lab"), None),
        P(("enc", "lab"), None, None),
    )
    out_specs = (P("lab", None), P(("enc", "lab"), None))
    return jax.shard_map(shards, mesh=mesh, in_specs=in_specs, out_specs=out_specs, check_vma=False)
```
